32 devices in a mesh: groups: 2 (over y), ctx: 4 (over z), dp: 2 (over x), tp: 2 (over core).
Axes of the slice: x: 2, y: 2, z: 4, core: 2. Of those that a mesh axis runs over, the one named last changes fastest.
Arguments:
- queries: bfloat16 [4, 1280, 2048], P(('groups', 'dp'), 'ctx', 'tp'), parts along dimension 0, may hold values from -6 to 6
- key_vectors: bfloat16 [4, 1280, 2048], P(('groups', 'dp'), 'ctx', 'tp'), parts along dimension 0, may hold values from -6 to 6
- value_vectors: bfloat16 [4, 1280, 2048], P(('groups', 'dp'), 'ctx', 'tp'), parts along dimension 0, may hold values from -6 to 6
- grad_output: bfloat16 [4, 1280, 2048], P(('groups', 'dp'), 'ctx', 'tp'), parts along dimension 0, may hold values from -6 to 6
Outputs:
- normed_out: bfloat16 [4, 1280, 2048], P(('groups', 'dp'), 'ctx', 'tp'), parts along dimension 0
- grad_queries: bfloat16 [4, 1280, 2048], P(('groups', 'dp'), 'ctx', 'tp'), parts along dimension 0
- grad_keys: bfloat16 [4, 1280, 2048], P(('groups', 'dp'), 'ctx', 'tp'), parts along dimension 0
- grad_values: bfloat16 [4, 1280, 2048], P(('groups', 'dp'), 'ctx', 'tp'), parts along dimension 0
The draws below stay inside these ranges and needn't reach their ends.
There are 2 independent parts, one for each index of `groups`. The reference program is written for one: setup_inputs(seed, part) draws one part's arguments, and reference() takes and returns one part's arrays. A program takes and returns all parts, laid end to end along the dimension named above; each array names one. Nothing has to cross between parts.
All inputs are finite; a program needn't handle non-finite values.
Results may differ from the reference program's by a relative error of at most 0.0059.
Values may be sent and summed in bfloat16 or wider, within the bound.
No kernel may reach another device: no remote copies, remote signals or barrier semaphores. Data moves between devices by JAX's collectives and lax.ppermute only.
A program may use at most 64 MiB of HBM per device.

```python
import jax
import jax.numpy as jnp
from jax import lax

DH = 128
BLOCK = 320
BATCH = 2
SEQ = 1280
WIDTH = 2048


def shard_levels(key, shape, cuts, low, largest):
    def one(position, parts):
        heights = jax.random.uniform(jax.random.fold_in(jax.random.fold_in(key, 6), position), (parts,), jnp.float32, low / len(cuts), largest / len(cuts))
        return jnp.repeat(jnp.exp(heights), shape[position] // parts).reshape((-1,) + (1,) * (len(shape) - position - 1))

    level = one(*cuts[0])
    for cut in cuts[1:]:
        level = level * one(*cut)
    return level


def bell_draw(own_key, extent, spread, limit, pieces=(), kind=jnp.bfloat16):
    factor_of = shard_levels(own_key, extent, pieces, -0.22, 0.18) if pieces else 1.0
    values = jax.random.normal(own_key, extent, jnp.float32) * spread * factor_of
    return jnp.minimum(jnp.maximum(values, -limit), limit).astype(kind)


def setup_inputs(seed: int = 0, part: int = 0) -> dict:
    arg_keys = jax.random.split(jax.random.key(seed), 5)
    own_keys = jax.random.split(jax.random.fold_in(arg_keys[4], part), 5)
    queries = bell_draw(own_keys[0], (BATCH, SEQ, WIDTH), 1.0, 6.0, ((0, 2), (1, 4), (2, 2)))
    key_vectors = bell_draw(own_keys[1], (BATCH, SEQ, WIDTH), 1.0, 6.0, ((0, 2), (1, 4), (2, 2)))
    value_vectors = bell_draw(own_keys[2], (BATCH, SEQ, WIDTH), 1.0, 6.0, ((0, 2), (1, 4), (2, 2)))
    grad_output = bell_draw(own_keys[3], (BATCH, SEQ, WIDTH), 1.0, 6.0, ((0, 2), (1, 4), (2, 2)))
    return dict(queries=queries, key_vectors=key_vectors, value_vectors=value_vectors, grad_output=grad_output)


norm_eps = 1e-06

def rounded(array):
    return lax.optimization_barrier(array.astype(jnp.bfloat16)).astype(jnp.float32)

def causal_mask(length):
    rows = lax.broadcasted_iota(jnp.int32, (length, length), 0)
    columns = lax.broadcasted_iota(jnp.int32, (length, length), 1)
    return columns <= rows

def block_scores(query_rows, key_rows):
    scores = jnp.einsum('thd,shd->hts', query_rows.astype(jnp.float32), key_rows.astype(jnp.float32))
    return rounded(jnp.where(causal_mask(query_rows.shape[0])[None], scores, 0.0))

def forward_block(inputs):
    query_rows, key_rows, value_rows, grad_rows, earlier = inputs
    query_f = query_rows.astype(jnp.float32)
    scores_low = block_scores(query_rows, key_rows)
    mixed = jnp.einsum('hts,she->the', scores_low, value_rows.astype(jnp.float32))
    mixed = mixed + jnp.einsum('thd,hde->the', query_f, rounded(earlier))
    inverse = lax.rsqrt(lax.optimization_barrier(jnp.mean(mixed * mixed, axis=-1, keepdims=True)) + norm_eps)
    normed = mixed * inverse
    grad_f = grad_rows.astype(jnp.float32)
    grad_mixed = inverse * (grad_f - normed * lax.optimization_barrier(jnp.mean(grad_f * normed, axis=-1, keepdims=True)))
    grad_low = rounded(grad_mixed)
    grad_state = jnp.einsum('thd,the->hde', query_f, grad_low)
    return (normed.astype(jnp.bfloat16), grad_low.astype(jnp.bfloat16), grad_state)

def backward_block(inputs):
    query_rows, key_rows, value_rows, grad_low, earlier, later = inputs
    query_f = query_rows.astype(jnp.float32)
    key_f = key_rows.astype(jnp.float32)
    value_f = value_rows.astype(jnp.float32)
    grad_f = grad_low.astype(jnp.float32)
    scores_low = block_scores(query_rows, key_rows)
    raw_grad = jnp.einsum('the,she->hts', grad_f, value_f)
    grad_scores = rounded(jnp.where(causal_mask(query_rows.shape[0])[None], raw_grad, 0.0))
    later_low = rounded(later)
    grad_q = jnp.einsum('hts,shd->thd', grad_scores, key_f) + jnp.einsum('the,hde->thd', grad_f, rounded(earlier))
    grad_k = jnp.einsum('hts,thd->shd', grad_scores, query_f) + jnp.einsum('she,hde->shd', value_f, later_low)
    grad_v = jnp.einsum('hts,the->she', scores_low, grad_f) + jnp.einsum('shd,hde->she', key_f, later_low)
    return (grad_q.astype(jnp.bfloat16), grad_k.astype(jnp.bfloat16), grad_v.astype(jnp.bfloat16))

def reference(queries, key_vectors, value_vectors, grad_output):
    batch_count, seq_len, width_all = queries.shape
    head_count = width_all // DH
    block_count = seq_len // BLOCK

    def blocks(array):
        return array.reshape(batch_count * block_count, BLOCK, head_count, DH)
    query_b = blocks(queries)
    key_b = blocks(key_vectors)
    value_b = blocks(value_vectors)
    grad_b = blocks(grad_output)
    state = jnp.einsum('nshd,nshe->nhde', key_b.astype(jnp.float32), value_b.astype(jnp.float32))
    state = state.reshape(batch_count, block_count, head_count, DH, DH)
    running = jnp.cumsum(state, axis=1)
    zero_block = jnp.zeros((batch_count, 1, head_count, DH, DH), jnp.float32)
    earlier = jnp.concatenate([zero_block, running[:, :-1]], axis=1)
    earlier_flat = earlier.reshape(batch_count * block_count, head_count, DH, DH)
    normed, grad_low, grad_state = lax.map(forward_block, (query_b, key_b, value_b, grad_b, earlier_flat))
    grad_state = grad_state.reshape(batch_count, block_count, head_count, DH, DH)
    behind = jnp.cumsum(grad_state[:, ::-1], axis=1)[:, ::-1]
    later = jnp.concatenate([behind[:, 1:], zero_block], axis=1)
    later_flat = later.reshape(batch_count * block_count, head_count, DH, DH)
    grad_q, grad_k, grad_v = lax.map(backward_block, (query_b, key_b, value_b, grad_low, earlier_flat, later_flat))

    def whole(array):
        return array.reshape(batch_count, seq_len, width_all)
    return (whole(normed), whole(grad_q), whole(grad_k), whole(grad_v))
```

```python
import jax
import jax.numpy as jnp
from jax import lax
from jax.experimental import pallas as pl
from jax.experimental.pallas import tpu as pltpu
from jax.sharding import PartitionSpec as P

DH = 128
norm_eps = 1e-06
F32 = jnp.float32
BF16 = jnp.bfloat16

VMEM_SPEC = pl.BlockSpec(memory_space=pltpu.VMEM)
ANY_SPEC = pl.BlockSpec(memory_space=pl.ANY)
PARAMS = pltpu.CompilerParams(vmem_limit_bytes=48 << 20)


def dot_nn(a, b):
    return lax.dot_general(a, b, (((1,), (0,)), ((), ())), preferred_element_type=F32)


def dot_nt(a, b):
    return lax.dot_general(a, b, (((1,), (1,)), ((), ())), preferred_element_type=F32)


def dot_tn(a, b):
    return lax.dot_general(a, b, (((0,), (0,)), ((), ())), preferred_element_type=F32)


def head(index):
    return slice(index * DH, (index + 1) * DH)


def causal(length):
    rows = lax.broadcasted_iota(jnp.int32, (length, length), 0)
    columns = lax.broadcasted_iota(jnp.int32, (length, length), 1)
    return columns <= rows


def state_kernel(order_ref, k_ref, v_ref, first_ref, second_ref):
    half_heads = first_ref.shape[0] // DH
    for place, out_ref in enumerate((first_ref, second_ref)):
        base = order_ref[place] * half_heads
        for h in range(half_heads):
            cols = pl.ds(pl.multiple_of((base + h) * DH, DH), DH)
            out_ref[head(h), :] = dot_tn(k_ref[:, cols], v_ref[:, cols]).astype(BF16)


def states(order, k, v):
    half_rows = k.shape[1] // 2
    shape = jax.ShapeDtypeStruct((half_rows, DH), BF16)
    return pl.pallas_call(
        state_kernel,
        out_shape=(shape, shape),
        in_specs=[pl.BlockSpec(memory_space=pltpu.SMEM), VMEM_SPEC, VMEM_SPEC],
        out_specs=(VMEM_SPEC, VMEM_SPEC),
        compiler_params=PARAMS,
        name="states",
    )(order, k, v)


def intra_kernel(q_ref, k_ref, v_ref, out_ref):
    mask = causal(q_ref.shape[0])
    for h in range(q_ref.shape[1] // DH):
        scores = dot_nt(q_ref[:, head(h)], k_ref[:, head(h)])
        scores = jnp.where(mask, scores, 0.0).astype(BF16)
        out_ref[:, head(h)] = dot_nn(scores, v_ref[:, head(h)])


def intra(q, k, v):
    length, width = q.shape
    steps = 2
    spec = pl.BlockSpec((length, width // steps), lambda i: (0, i))
    return pl.pallas_call(
        intra_kernel,
        out_shape=jax.ShapeDtypeStruct(q.shape, F32),
        grid=(steps,),
        in_specs=[spec] * 3,
        out_specs=spec,
        compiler_params=PARAMS,
        cost_estimate=pl.CostEstimate(flops=4 * length * length * width, transcendentals=0, bytes_accessed=10 * length * width),
        name="intra",
    )(q, k, v)


def mid_kernel(half_ref, q_ref, g_ref, intra_ref, e_ref, *refs):
    normed_ref, grad_ref, state_ref = refs[-3:]
    for h in range(q_ref.shape[1] // DH):
        q = q_ref[:, head(h)]
        mixed = intra_ref[:, head(h)] + dot_nn(q, e_ref[head(h), :])
        inverse = lax.rsqrt(jnp.mean(mixed * mixed, axis=-1, keepdims=True) + norm_eps)
        normed = mixed * inverse
        g = g_ref[:, head(h)].astype(F32)
        grad = inverse * (g - normed * jnp.mean(g * normed, axis=-1, keepdims=True))
        grad = grad.astype(BF16)
        normed_ref[:, head(h)] = normed.astype(BF16)
        grad_ref[:, head(h)] = grad
        state_ref[head(h), :] = dot_tn(q, grad).astype(BF16)


def mid(half, q, g, intra_out, earlier, filled=None):
    length, width = q.shape
    columns = pl.BlockSpec((length, width // 2), lambda i, half: (0, half[0]))
    whole = pl.BlockSpec(earlier.shape, lambda i, half: (0, 0))
    extra = () if filled is None else filled
    return pl.pallas_call(
        mid_kernel,
        out_shape=(
            jax.ShapeDtypeStruct(q.shape, BF16),
            jax.ShapeDtypeStruct(q.shape, BF16),
            jax.ShapeDtypeStruct(earlier.shape, BF16),
        ),
        grid_spec=pltpu.PrefetchScalarGridSpec(
            num_scalar_prefetch=1,
            grid=(1,),
            in_specs=[columns, columns, columns, whole] + [ANY_SPEC] * len(extra),
            out_specs=(columns, columns, whole),
        ),
        input_output_aliases={5: 0, 6: 1} if extra else {},
        compiler_params=PARAMS,
        cost_estimate=pl.CostEstimate(flops=2 * length * width * DH, transcendentals=0, bytes_accessed=6 * length * width),
        name="mid",
    )(half, q, g, intra_out, earlier, *extra)


def back_kernel(half_ref, q_ref, k_ref, v_ref, grad_ref, e0_ref, e1_ref, gq_ref, gk_ref, gv_ref):
    mask = causal(q_ref.shape[0])
    early = pl.program_id(0) == half_ref[0]
    for h in range(q_ref.shape[1] // DH):
        q, k, v, grad = (ref[:, head(h)] for ref in (q_ref, k_ref, v_ref, grad_ref))
        e = jnp.where(early, e0_ref[head(h), :], e1_ref[head(h), :])
        scores = jnp.where(mask, dot_nt(q, k), 0.0).astype(BF16)
        grad_scores = jnp.where(mask, dot_nt(grad, v), 0.0).astype(BF16)
        gq_ref[:, head(h)] = (dot_nn(grad_scores, k) + dot_nt(grad, e)).astype(BF16)
        gk_ref[:, head(h)] = dot_tn(grad_scores, q)
        gv_ref[:, head(h)] = dot_tn(scores, grad)


def back(half, q, k, v, grad, e_first, e_second):
    length, width = q.shape
    columns = pl.BlockSpec((length, width // 2), lambda i, half: (0, i))
    whole = pl.BlockSpec(e_first.shape, lambda i, half: (0, 0))
    return pl.pallas_call(
        back_kernel,
        out_shape=(
            jax.ShapeDtypeStruct(q.shape, BF16),
            jax.ShapeDtypeStruct(q.shape, F32),
            jax.ShapeDtypeStruct(q.shape, F32),
        ),
        grid_spec=pltpu.PrefetchScalarGridSpec(
            num_scalar_prefetch=1,
            grid=(2,),
            in_specs=[columns] * 4 + [whole] * 2,
            out_specs=(columns,) * 3,
        ),
        compiler_params=PARAMS,
        cost_estimate=pl.CostEstimate(flops=10 * length * length * width, transcendentals=0, bytes_accessed=18 * length * width),
        name="back",
    )(half, q, k, v, grad, e_first, e_second)


def post_kernel(half_ref, k_ref, v_ref, gk_in_ref, gv_in_ref, l_ref, *refs):
    gk_ref, gv_ref = refs[-2:]
    for h in range(k_ref.shape[1] // DH):
        later = l_ref[head(h), :]
        gk_ref[:, head(h)] = (gk_in_ref[:, head(h)] + dot_nt(v_ref[:, head(h)], later)).astype(BF16)
        gv_ref[:, head(h)] = (gv_in_ref[:, head(h)] + dot_nn(k_ref[:, head(h)], later)).astype(BF16)


def post(half, k, v, gk_in, gv_in, later, filled=None):
    length, width = k.shape
    columns = pl.BlockSpec((length, width // 2), lambda i, half: (0, half[0]))
    whole = pl.BlockSpec(later.shape, lambda i, half: (0, 0))
    extra = () if filled is None else filled
    return pl.pallas_call(
        post_kernel,
        out_shape=(jax.ShapeDtypeStruct(k.shape, BF16), jax.ShapeDtypeStruct(k.shape, BF16)),
        grid_spec=pltpu.PrefetchScalarGridSpec(
            num_scalar_prefetch=1,
            grid=(1,),
            in_specs=[columns] * 4 + [whole] + [ANY_SPEC] * len(extra),
            out_specs=(columns, columns),
        ),
        input_output_aliases={6: 0, 7: 1} if extra else {},
        compiler_params=PARAMS,
        cost_estimate=pl.CostEstimate(flops=2 * length * width * DH, transcendentals=0, bytes_accessed=8 * length * width),
        name="post",
    )(half, k, v, gk_in, gv_in, later, *extra)


def index(value):
    return jnp.asarray(value, jnp.int32).reshape(1)


def shards_four(queries, key_vectors, value_vectors, grad_output):
    out_shape = queries.shape
    q, k, v, g = (x.reshape(x.shape[1:]) for x in (queries, key_vectors, value_vectors, grad_output))
    me = lax.axis_index("ctx")

    def send(x, pairs):
        return lax.ppermute(x, "ctx", pairs)

    flip = jnp.where(me == 0, 0, 1).astype(jnp.int32)
    s1, s2 = states(jnp.stack([flip, 1 - flip]), k, v)
    r1 = send(s1, [(0, 1), (1, 2)])
    r2 = send(s2, [(0, 2), (2, 1)])
    intra_out = intra(q, k, v)
    f1, f2, fs1, fs2 = (x.astype(F32) for x in (r1, r2, s1, s2))
    s3 = (f1 + jnp.where(me == 1, fs2, f2 + fs1)).astype(BF16)
    s4 = (f2 + jnp.where(me == 1, f1 + fs2, 0.0)).astype(BF16)
    r3 = send(s3, [(1, 2), (2, 3)])
    r4 = send(s4, [(1, 3), (2, 1)])
    e_early = jnp.where(me == 1, r1, r3)
    h_early = index(jnp.where(me == 3, 1, 0))
    normed, grad, g_early = mid(h_early, q, g, intra_out, e_early)
    u1 = send(g_early, [(3, 2), (2, 1)])
    e_late = jnp.where(me == 2, (f1 + f2).astype(BF16), r4)
    normed, grad, g_late = mid(1 - h_early, q, g, intra_out, e_late, (normed, grad))
    u2 = send(g_late, [(3, 1), (1, 2)])
    grad_q, gk_in, gv_in = back(h_early, q, k, v, grad, e_early, e_late)
    f1, f2, fe, fl = (x.astype(F32) for x in (u1, u2, g_early, g_late))
    t3 = (f1 + jnp.where(me == 2, fl, f2 + fe)).astype(BF16)
    t4 = (f2 + jnp.where(me == 2, f1 + fl, 0.0)).astype(BF16)
    w3 = send(t3, [(2, 1), (1, 0)])
    w4 = send(t4, [(2, 0), (1, 2)])
    l_early = jnp.where(me == 2, u1, w3)
    p_early = index(jnp.where(me == 0, 0, 1))
    grad_k, grad_v = post(p_early, k, v, gk_in, gv_in, l_early)
    l_late = jnp.where(me == 1, (f1 + f2).astype(BF16), w4)
    grad_k, grad_v = post(1 - p_early, k, v, gk_in, gv_in, l_late, (grad_k, grad_v))
    return tuple(x.reshape(out_shape) for x in (normed, grad_q, grad_k, grad_v))


def scan_states(first, second, count, backward):
    rows = first.shape[0] * 2
    shares = jnp.concatenate([first, second], axis=0).reshape(count, rows // count, DH)
    shares = lax.all_to_all(shares, "ctx", split_axis=0, concat_axis=0, tiled=True).astype(F32)
    running = jnp.cumsum(shares, axis=0)
    sums = running[-1:] - running if backward else running - shares
    sums = lax.all_to_all(sums.astype(BF16), "ctx", split_axis=0, concat_axis=0, tiled=True)
    sums = sums.reshape(rows, DH)
    return sums[: rows // 2], sums[rows // 2 :]


def shards_any(count, queries, key_vectors, value_vectors, grad_output):
    out_shape = queries.shape
    q, k, v, g = (x.reshape(x.shape[1:]) for x in (queries, key_vectors, value_vectors, grad_output))
    s1, s2 = states(jnp.array([0, 1], jnp.int32), k, v)
    e1, e2 = scan_states(s1, s2, count, False)
    intra_out = intra(q, k, v)
    low, high = index(0), index(1)
    normed, grad, g1 = mid(low, q, g, intra_out, e1)
    normed, grad, g2 = mid(high, q, g, intra_out, e2, (normed, grad))
    l1, l2 = scan_states(g1, g2, count, True)
    grad_q, gk_in, gv_in = back(low, q, k, v, grad, e1, e2)
    grad_k, grad_v = post(low, k, v, gk_in, gv_in, l1)
    grad_k, grad_v = post(high, k, v, gk_in, gv_in, l2, (grad_k, grad_v))
    return tuple(x.reshape(out_shape) for x in (normed, grad_q, grad_k, grad_v))


def solution(mesh):
    placed = P(("groups", "dp"), "ctx", "tp")
    count = mesh.shape["ctx"]

    def shards(*args):
        if count == 4:
            return shards_four(*args)
        return shards_any(count, *args)

    return jax.shard_map(
        shards,
        mesh=mesh,
        in_specs=(placed,) * 4,
        out_specs=(placed,) * 4,
        check_vma=False,
    )
```

```python
import functools

import jax
import jax.numpy as jnp
from jax import lax
from jax.experimental import pallas as pl
from jax.experimental.pallas import tpu as pltpu
from jax.sharding import PartitionSpec as P

DH = 128
norm_eps = 1e-06
F32 = jnp.float32
BF16 = jnp.bfloat16

VMEM_SPEC = pl.BlockSpec(memory_space=pltpu.VMEM)
HBM_SPEC = pl.BlockSpec(memory_space=pltpu.HBM)
SMEM_SPEC = pl.BlockSpec(memory_space=pltpu.SMEM)
PARAMS = pltpu.CompilerParams(vmem_limit_bytes=16 << 20)


def cost(flops, moved):
    return pl.CostEstimate(flops=flops, transcendentals=0, bytes_accessed=moved)


def dot_nn(a, b):
    return lax.dot_general(a, b, (((1,), (0,)), ((), ())), preferred_element_type=F32)


def dot_nt(a, b):
    return lax.dot_general(a, b, (((1,), (1,)), ((), ())), preferred_element_type=F32)


def dot_tn(a, b):
    return lax.dot_general(a, b, (((0,), (0,)), ((), ())), preferred_element_type=F32)


def head(index):
    return slice(index * DH, (index + 1) * DH)


def causal(length):
    rows = lax.broadcasted_iota(jnp.int32, (length, length), 0)
    columns = lax.broadcasted_iota(jnp.int32, (length, length), 1)
    return columns <= rows


def half_columns(half, h, heads):
    return pl.ds(pl.multiple_of((half * heads + h) * DH, DH), DH)


def load_kernel(half_of, me_ref, k_ref, v_ref, out_ref, k_out, v_out, k_sem, v_sem):
    heads = out_ref.shape[0] // DH
    half = half_of(me_ref[0])
    copies = []
    for h in range(2 * heads):
        cols = half_columns(half if h < heads else 1 - half, h % heads, heads)
        pair = (
            pltpu.make_async_copy(k_ref.at[:, cols], k_out.at[:, cols], k_sem.at[h]),
            pltpu.make_async_copy(v_ref.at[:, cols], v_out.at[:, cols], v_sem.at[h]),
        )
        for copy in pair:
            copy.start()
        copies.append((cols, pair))
    for h, (cols, pair) in enumerate(copies):
        for copy in pair:
            copy.wait()
        if h < heads:
            out_ref[head(h), :] = dot_tn(k_out[:, cols], v_out[:, cols]).astype(BF16)


def load_states(half_of, me, k, v):
    length, width = k.shape
    heads = width // DH
    k, v = (pltpu.with_memory_space_constraint(x, pltpu.HBM) for x in (k, v))
    whole = jax.ShapeDtypeStruct(k.shape, BF16)
    return pl.pallas_call(
        functools.partial(load_kernel, half_of),
        out_shape=(jax.ShapeDtypeStruct((width // 2, DH), BF16), whole, whole),
        in_specs=[SMEM_SPEC, HBM_SPEC, HBM_SPEC],
        out_specs=(VMEM_SPEC,) * 3,
        scratch_shapes=[pltpu.SemaphoreType.DMA((heads,))] * 2,
        compiler_params=PARAMS,
        cost_estimate=cost(length * width * DH, 8 * length * width),
        name="load_states",
    )(me, k, v)


def state_kernel(half_of, me_ref, k_ref, v_ref, out_ref):
    heads = out_ref.shape[0] // DH
    half = half_of(me_ref[0])
    for h in range(heads):
        cols = half_columns(half, h, heads)
        out_ref[head(h), :] = dot_tn(k_ref[:, cols], v_ref[:, cols]).astype(BF16)


def states(half_of, me, k, v):
    length, width = k.shape
    return pl.pallas_call(
        functools.partial(state_kernel, half_of),
        out_shape=jax.ShapeDtypeStruct((width // 2, DH), BF16),
        in_specs=[SMEM_SPEC, VMEM_SPEC, VMEM_SPEC],
        out_specs=VMEM_SPEC,
        compiler_params=PARAMS,
        cost_estimate=cost(length * width * DH, 2 * length * width),
        name="states",
    )(me, k, v)


def intra_kernel(q_ref, k_ref, v_ref, out_ref, qt_ref, token_ref):
    mask = causal(q_ref.shape[0])
    for h in range(q_ref.shape[1] // DH):
        q = q_ref[:, head(h)]
        scores = jnp.where(mask, dot_nt(q, k_ref[:, head(h)]), 0.0).astype(BF16)
        out_ref[:, head(h)] = dot_nn(scores, v_ref[:, head(h)])
        qt_ref[head(h), :] = q.T
    token_ref[...] = jnp.zeros_like(token_ref)


TOKEN = jax.ShapeDtypeStruct((8, DH), F32)


def intra(q, k, v):
    length, width = q.shape
    return pl.pallas_call(
        intra_kernel,
        out_shape=(jax.ShapeDtypeStruct(q.shape, F32), jax.ShapeDtypeStruct((width, length), BF16), TOKEN),
        in_specs=[VMEM_SPEC] * 3,
        out_specs=(VMEM_SPEC,) * 3,
        compiler_params=PARAMS,
        cost_estimate=cost(4 * length * length * width, 12 * length * width),
        name="intra",
    )(q, k, v)


def add_kernel(a_ref, b_ref, token_ref, out_ref):
    out_ref[...] = (a_ref[...].astype(F32) + b_ref[...].astype(F32)).astype(BF16)


def add(a, b, token):
    return pl.pallas_call(
        add_kernel,
        out_shape=jax.ShapeDtypeStruct(a.shape, BF16),
        in_specs=[VMEM_SPEC] * 3,
        out_specs=VMEM_SPEC,
        compiler_params=PARAMS,
        cost_estimate=cost(a.size, 6 * a.size),
        name="add",
    )(a, b, token)


def combine_kernel(turn, me_ref, r1_ref, r2_ref, a_ref, b_ref, token_ref, x_ref, y_ref, both_ref):
    near = me_ref[0] == turn
    r1, r2, a, b = (ref[...].astype(F32) for ref in (r1_ref, r2_ref, a_ref, b_ref))
    x_ref[...] = (r1 + r2 + a).astype(BF16)
    y_ref[...] = (r2 + jnp.where(near, r1 + b, 0.0)).astype(BF16)
    both_ref[...] = (r1 + r2).astype(BF16)


def combine(turn, me, r1, r2, a, b, token):
    shape = jax.ShapeDtypeStruct(r1.shape, BF16)
    return pl.pallas_call(
        functools.partial(combine_kernel, turn),
        out_shape=(shape,) * 3,
        in_specs=[SMEM_SPEC] + [VMEM_SPEC] * 5,
        out_specs=(VMEM_SPEC,) * 3,
        compiler_params=PARAMS,
        cost_estimate=cost(r1.size, 10 * r1.size),
        name="combine",
    )(me, r1, r2, a, b, token)


def pick(me, choices, refs, rows):
    value = refs[-1][rows, :]
    for turn, ref in zip(choices, refs[:-1]):
        value = jnp.where(me == turn, ref[rows, :], value)
    return value


def mid_kernel(half_of, turns, me_ref, q_ref, qt_ref, g_ref, intra_ref, token_ref, *refs):
    e_refs, (normed_ref, grad_ref, state_ref, done_ref) = refs[:-4], refs[-4:]
    heads = state_ref.shape[0] // DH
    half = half_of(me_ref[0])
    for h in range(heads):
        cols = half_columns(half, h, heads)
        earlier = pick(me_ref[0], turns, e_refs, head(h))
        mixed = intra_ref[:, cols] + dot_nn(q_ref[:, cols], earlier)
        g = g_ref[:, cols].astype(F32)
        inverse = lax.rsqrt(jnp.mean(mixed * mixed, axis=-1, keepdims=True) + norm_eps)
        along = jnp.mean(g * mixed, axis=-1, keepdims=True) * inverse
        normed = mixed * inverse
        grad = (inverse * (g - normed * along)).astype(BF16)
        grad_ref[:, head(h)] = grad
        state_ref[head(h), :] = dot_nn(qt_ref[cols, :], grad).astype(BF16)
        normed_ref[:, head(h)] = normed.astype(BF16)
    done_ref[...] = jnp.zeros_like(done_ref)


def mid(half_of, turns, me, q, qt, g, intra_out, token, earlier):
    length, width = q.shape
    half_shape = jax.ShapeDtypeStruct((length, width // 2), BF16)
    return pl.pallas_call(
        functools.partial(mid_kernel, half_of, turns),
        out_shape=(half_shape, half_shape, jax.ShapeDtypeStruct(earlier[0].shape, BF16), TOKEN),
        in_specs=[SMEM_SPEC] + [VMEM_SPEC] * (5 + len(earlier)),
        out_specs=(VMEM_SPEC,) * 4,
        compiler_params=PARAMS,
        cost_estimate=cost(2 * length * width * DH, 6 * length * width),
        name="mid",
    )(me, q, qt, g, intra_out, token, *earlier)


def back_kernel(half_of, turns, me_ref, q_ref, k_ref, v_ref, grad_ref, normed_in_ref, *refs):
    e_refs, (normed_ref, gq_ref, gk_ref, gv_ref, token_ref, gq_buf, gq_sem, normed_sem) = refs[: len(turns) + 1], refs[-8:]
    length = q_ref.shape[0]
    rows = lax.broadcasted_iota(jnp.int32, (length, length), 0)
    columns = lax.broadcasted_iota(jnp.int32, (length, length), 1)
    mask, mask_t = columns <= rows, rows <= columns
    heads = gk_ref.shape[1] // DH
    half = half_of(me_ref[0])
    copies = []
    for h in range(heads):
        cols = half_columns(half, h, heads)
        copies.append(pltpu.make_async_copy(normed_in_ref.at[:, head(h)], normed_ref.at[:, cols], normed_sem.at[h]))
        copies[-1].start()
    for h in range(heads):
        cols = half_columns(half, h, heads)
        q, k, v = (ref[:, cols] for ref in (q_ref, k_ref, v_ref))
        grad = grad_ref[:, head(h)]
        earlier = pick(me_ref[0], turns, e_refs, head(h))
        scores_t = jnp.where(mask_t, dot_nt(k, q), 0.0).astype(BF16)
        grad_scores = jnp.where(mask, dot_nt(grad, v), 0.0).astype(BF16)
        grad_scores_t = jnp.where(mask_t, dot_nt(v, grad), 0.0).astype(BF16)
        gq_buf[h] = (dot_nn(grad_scores, k) + dot_nt(grad, earlier)).astype(BF16)
        copies.append(pltpu.make_async_copy(gq_buf.at[h], gq_ref.at[:, cols], gq_sem.at[h]))
        copies[-1].start()
        gk_ref[:, head(h)] = dot_nn(grad_scores_t, q)
        gv_ref[:, head(h)] = dot_nn(scores_t, grad)
    token_ref[...] = jnp.zeros_like(token_ref)
    for copy in copies:
        copy.wait()


def back(half_of, turns, me, q, k, v, grad, normed, earlier, filled=()):
    length, width = q.shape
    heads = width // (2 * DH)
    whole = jax.ShapeDtypeStruct(q.shape, BF16)
    half_shape = jax.ShapeDtypeStruct((length, width // 2), F32)
    first_filled = 6 + len(earlier)
    return pl.pallas_call(
        functools.partial(back_kernel, half_of, turns),
        out_shape=(whole, whole, half_shape, half_shape, TOKEN),
        in_specs=[SMEM_SPEC] + [VMEM_SPEC] * (5 + len(earlier)) + [HBM_SPEC] * len(filled),
        out_specs=(HBM_SPEC, HBM_SPEC, VMEM_SPEC, VMEM_SPEC, VMEM_SPEC),
        scratch_shapes=[pltpu.VMEM((heads, length, DH), BF16)] + [pltpu.SemaphoreType.DMA((heads,))] * 2,
        input_output_aliases={first_filled: 0, first_filled + 1: 1} if filled else {},
        compiler_params=PARAMS,
        cost_estimate=cost(6 * length * length * width, 9 * length * width),
        name="back",
    )(me, q, k, v, grad, normed, *earlier, *filled)


def post_kernel(half_of, turns, me_ref, k_ref, v_ref, gk_in_ref, gv_in_ref, token_ref, *refs):
    l_refs, (gk_ref, gv_ref, gk_buf, gv_buf, gk_sem, gv_sem) = refs[: len(turns) + 1], refs[-6:]
    heads = gk_in_ref.shape[1] // DH
    half = half_of(me_ref[0])
    copies = []
    for h in range(heads):
        cols = half_columns(half, h, heads)
        later = pick(me_ref[0], turns, l_refs, head(h))
        gk_buf[h] = (gk_in_ref[:, head(h)] + dot_nt(v_ref[:, cols], later)).astype(BF16)
        copies.append(pltpu.make_async_copy(gk_buf.at[h], gk_ref.at[:, cols], gk_sem.at[h]))
        copies[-1].start()
        gv_buf[h] = (gv_in_ref[:, head(h)] + dot_nn(k_ref[:, cols], later)).astype(BF16)
        copies.append(pltpu.make_async_copy(gv_buf.at[h], gv_ref.at[:, cols], gv_sem.at[h]))
        copies[-1].start()
    for copy in copies:
        copy.wait()


def post(half_of, turns, me, k, v, gk_in, gv_in, token, later, filled=()):
    length, width = k.shape
    heads = width // (2 * DH)
    first_filled = 6 + len(later)
    return pl.pallas_call(
        functools.partial(post_kernel, half_of, turns),
        out_shape=(jax.ShapeDtypeStruct(k.shape, BF16), jax.ShapeDtypeStruct(k.shape, BF16)),
        in_specs=[SMEM_SPEC] + [VMEM_SPEC] * (5 + len(later)) + [HBM_SPEC] * len(filled),
        out_specs=(HBM_SPEC, HBM_SPEC),
        scratch_shapes=[pltpu.VMEM((heads, length, DH), BF16)] * 2 + [pltpu.SemaphoreType.DMA((heads,))] * 2,
        input_output_aliases={first_filled: 0, first_filled + 1: 1} if filled else {},
        compiler_params=PARAMS,
        cost_estimate=cost(2 * length * width * DH, 8 * length * width),
        name="post",
    )(me, k, v, gk_in, gv_in, token, *later, *filled)


def ends_half(me):
    return jnp.where((me == 0) | (me == 3), 1, 0)


def inner_half(me):
    return 1 - ends_half(me)


def zero_half(me):
    return jnp.where(me == 0, 0, 1)


def rest_half(me):
    return 1 - zero_half(me)


def rows_of(array):
    return array.reshape(array.shape[1:])


def shards_four(queries, key_vectors, value_vectors, grad_output):
    out_shape = queries.shape
    q, k, v, g = (rows_of(x) for x in (queries, key_vectors, value_vectors, grad_output))
    me = lax.axis_index("ctx").astype(jnp.int32).reshape(1)

    def send(x, pairs):
        return lax.ppermute(x, "ctx", pairs)

    s1, k, v = load_states(zero_half, me, k, v)
    r1 = send(s1, [(0, 1), (1, 2)])
    s2 = states(rest_half, me, k, v)
    r2 = send(s2, [(0, 2), (2, 1)])
    intra_out, qt, token = intra(q, k, v)
    r3b = send(add(r1, s2, token), [(1, 2)])
    s3, s4, r12 = combine(1, me, r1, r2, s1, s2, token)
    r3a = send(s3, [(2, 3)])
    r4 = send(s4, [(1, 3), (2, 1)])
    e_early = (r1, r3b, r3a)
    e_late = (r12, r4)
    normed_early, grad_early, g_early, token = mid(ends_half, (1, 2), me, q, qt, g, intra_out, token, e_early)
    u1 = send(g_early, [(3, 2), (2, 1)])
    normed_late, grad_late, g_late, token = mid(inner_half, (2,), me, q, qt, g, intra_out, token, e_late)
    u2 = send(g_late, [(3, 1), (1, 2)])
    normed, grad_q, gk_late, gv_late, token = back(inner_half, (2,), me, q, k, v, grad_late, normed_late, e_late)
    w3b = send(add(u1, g_late, token), [(2, 1)])
    t3, t4, u12 = combine(2, me, u1, u2, g_early, g_late, token)
    w3a = send(t3, [(1, 0)])
    w4 = send(t4, [(2, 0), (1, 2)])
    normed, grad_q, gk_early, gv_early, token = back(
        ends_half, (1, 2), me, q, k, v, grad_early, normed_early, e_early, (normed, grad_q)
    )
    filled = post(inner_half, (2, 1), me, k, v, gk_late, gv_late, token, (u1, w3b, w3a))
    grad_k, grad_v = post(ends_half, (1,), me, k, v, gk_early, gv_early, token, (u12, w4), filled)
    return tuple(x.reshape(out_shape) for x in (normed, grad_q, grad_k, grad_v))


def scan_states(first, second, count, backward):
    rows = first.shape[0] * 2
    shares = jnp.concatenate([first, second], axis=0).reshape(count, rows // count, DH)
    shares = lax.all_to_all(shares, "ctx", split_axis=0, concat_axis=0, tiled=True).astype(F32)
    running = jnp.cumsum(shares, axis=0)
    sums = running[-1:] - running if backward else running - shares
    sums = lax.all_to_all(sums.astype(BF16), "ctx", split_axis=0, concat_axis=0, tiled=True)
    sums = sums.reshape(rows, DH)
    return sums[: rows // 2], sums[rows // 2 :]


def low_half(me):
    return 0


def high_half(me):
    return 1


def shards_any(count, queries, key_vectors, value_vectors, grad_output):
    out_shape = queries.shape
    q, k, v, g = (rows_of(x) for x in (queries, key_vectors, value_vectors, grad_output))
    me = lax.axis_index("ctx").astype(jnp.int32).reshape(1)
    s1, k, v = load_states(low_half, me, k, v)
    e1, e2 = scan_states(s1, states(high_half, me, k, v), count, False)
    intra_out, qt, token = intra(q, k, v)
    normed1, grad1, g1, token = mid(low_half, (), me, q, qt, g, intra_out, token, (e1,))
    normed2, grad2, g2, token = mid(high_half, (), me, q, qt, g, intra_out, token, (e2,))
    l1, l2 = scan_states(g1, g2, count, True)
    normed, grad_q, gk1, gv1, token = back(low_half, (), me, q, k, v, grad1, normed1, (e1,))
    normed, grad_q, gk2, gv2, token = back(high_half, (), me, q, k, v, grad2, normed2, (e2,), (normed, grad_q))
    filled = post(low_half, (), me, k, v, gk1, gv1, token, (l1,))
    grad_k, grad_v = post(high_half, (), me, k, v, gk2, gv2, token, (l2,), filled)
    return tuple(x.reshape(out_shape) for x in (normed, grad_q, grad_k, grad_v))


def solution(mesh):
    placed = P(("groups", "dp"), "ctx", "tp")
    count = mesh.shape["ctx"]

    def shards(*args):
        if count == 4:
            return shards_four(*args)
        return shards_any(count, *args)

    return jax.shard_map(
        shards,
        mesh=mesh,
        in_specs=(placed,) * 4,
        out_specs=(placed,) * 4,
        check_vma=False,
    )
```

```python
import functools

import jax
import jax.numpy as jnp
from jax import lax
from jax.experimental import pallas as pl
from jax.experimental.pallas import tpu as pltpu
from jax.sharding import PartitionSpec as P

DH = 128
norm_eps = 1e-06
F32 = jnp.float32
BF16 = jnp.bfloat16

VMEM_SPEC = pl.BlockSpec(memory_space=pltpu.VMEM)
HBM_SPEC = pl.BlockSpec(memory_space=pltpu.HBM)
SMEM_SPEC = pl.BlockSpec(memory_space=pltpu.SMEM)
COST = pl.CostEstimate(flops=0, transcendentals=0, bytes_accessed=4096)
PARAMS = pltpu.CompilerParams(vmem_limit_bytes=16 << 20)


def params(name, parts):
    return dict(compiler_params=PARAMS, cost_estimate=COST, name=name, out_shape=parts)


def dot_nn(a, b):
    return lax.dot_general(a, b, (((1,), (0,)), ((), ())), preferred_element_type=F32)


def dot_nt(a, b):
    return lax.dot_general(a, b, (((1,), (1,)), ((), ())), preferred_element_type=F32)


def dot_tn(a, b):
    return lax.dot_general(a, b, (((0,), (0,)), ((), ())), preferred_element_type=F32)


def head(index):
    return slice(index * DH, (index + 1) * DH)


def causal(length):
    rows = lax.broadcasted_iota(jnp.int32, (length, length), 0)
    columns = lax.broadcasted_iota(jnp.int32, (length, length), 1)
    return columns <= rows


def half_columns(half, h, heads):
    return pl.ds(pl.multiple_of((half * heads + h) * DH, DH), DH)


def among(me, roles):
    hit = me == roles[0]
    for role in roles[1:]:
        hit = hit | (me == role)
    return hit


def on(me, roles):
    return pl.when(among(me, roles)) if roles else lambda body: body()


def state_kernel(plan, duplicate, me_ref, k_ref, v_ref, token_ref, *refs):
    spare, outs = refs[: len(duplicate[:1])], refs[len(duplicate[:1]) : -5]
    done_ref, k_buf, v_buf, k_sem, v_sem = refs[-5:]
    heads = outs[0].shape[0] // DH
    done_ref[...] = token_ref[...]
    if duplicate:

        @on(me_ref[0], (duplicate[0],))
        def _():
            outs[duplicate[1]][...] = spare[0][...]

    for roles, pieces in plan:

        @on(me_ref[0], roles)
        def _():
            copies = []
            for half, out in pieces:
                for h in range(heads):
                    cols, slot = head(half * heads + h), len(copies)
                    pair = (
                        pltpu.make_async_copy(k_ref.at[:, cols], k_buf.at[slot], k_sem.at[slot]),
                        pltpu.make_async_copy(v_ref.at[:, cols], v_buf.at[slot], v_sem.at[slot]),
                    )
                    for copy in pair:
                        copy.start()
                    copies.append((outs[out], head(h), pair))
            for slot, (out_ref, rows, pair) in enumerate(copies):
                for copy in pair:
                    copy.wait()
                out_ref[rows, :] = dot_tn(k_buf[slot], v_buf[slot]).astype(BF16)


def states(plan, me, k, v, token, duplicate=(), spare=()):
    length, width = k.shape
    count = 1 + max(out for _, pieces in plan for _, out in pieces)
    slots = max(len(pieces) for _, pieces in plan) * width // (2 * DH)
    k, v = (pltpu.with_memory_space_constraint(x, pltpu.HBM) for x in (k, v))
    shape = jax.ShapeDtypeStruct((width // 2, DH), BF16)
    return pl.pallas_call(
        functools.partial(state_kernel, plan, duplicate),
        in_specs=[SMEM_SPEC, HBM_SPEC, HBM_SPEC] + [VMEM_SPEC] * (1 + len(spare)),
        out_specs=(VMEM_SPEC,) * (count + 1),
        scratch_shapes=[pltpu.VMEM((slots, length, DH), BF16)] * 2 + [pltpu.SemaphoreType.DMA((slots,))] * 2,
        **params("states", (shape,) * count + (TOKEN,)),
    )(me, k, v, token, *spare)


TOKEN = jax.ShapeDtypeStruct((8, DH), F32)


def intra_kernel(q_ref, k_ref, v_ref, token_ref, out_ref, qt_ref, done_ref):
    mask = causal(q_ref.shape[0])
    for h in range(q_ref.shape[1] // DH):
        q = q_ref[:, head(h)]
        scores = jnp.where(mask, dot_nt(q, k_ref[:, head(h)]), 0.0).astype(BF16)
        out_ref[:, head(h)] = dot_nn(scores, v_ref[:, head(h)])
        qt_ref[head(h), :] = q.T
    done_ref[...] = token_ref[...]


def intra(q, k, v, token):
    length, width = q.shape
    return pl.pallas_call(
        intra_kernel,
        in_specs=[VMEM_SPEC] * 4,
        out_specs=(VMEM_SPEC,) * 3,
        **params("intra", (jax.ShapeDtypeStruct(q.shape, F32), jax.ShapeDtypeStruct((width, length), BF16), TOKEN)),
    )(q, k, v, token)


def total(refs, rows=slice(None)):
    value = refs[0][rows, :].astype(F32)
    for ref in refs[1:]:
        value = value + ref[rows, :].astype(F32)
    return value.astype(BF16)


def add_kernel(token_ref, *refs):
    refs[-2][...] = total(refs[:-2])
    refs[-1][...] = token_ref[...]


def add(token, *arrays):
    return pl.pallas_call(
        add_kernel,
        in_specs=[VMEM_SPEC] * (1 + len(arrays)),
        out_specs=(VMEM_SPEC,) * 2,
        **params("add", (jax.ShapeDtypeStruct(arrays[0].shape, BF16), TOKEN)),
    )(token, *arrays)


def half_columns(half, h, heads):
    return pl.ds(pl.multiple_of((half * heads + h) * DH, DH), DH)


def mid_kernel(half_of, roles, keep, merge, me_ref, q_ref, qt_ref, g_ref, intra_ref, token_ref, *refs):
    normed_ref, grad_ref, earlier_ref, done_ref, *state_refs = refs[-5 - merge :]
    other, e_refs = refs[: len(keep) + merge], refs[len(keep) + merge : -5 - merge]
    state_ref = state_refs[0]
    heads = state_ref.shape[0] // DH
    done_ref[...] = token_ref[...]
    if keep:

        @on(me_ref[0], keep)
        def _():
            state_ref[...] = other[0][...]

    if merge:

        @pl.when(jnp.logical_not(among(me_ref[0], roles)))
        def _():
            state_refs[1][...] = other[-1][...]

    @on(me_ref[0], roles)
    def _():
        half = half_of(me_ref[0])
        for h in range(heads):
            cols = half_columns(half, h, heads)
            earlier = total(e_refs, head(h))
            earlier_ref[head(h), :] = earlier
            mixed = intra_ref[:, cols] + dot_nn(q_ref[:, cols], earlier)
            g = g_ref[:, cols].astype(F32)
            inverse = lax.rsqrt(jnp.mean(mixed * mixed, axis=-1, keepdims=True) + norm_eps)
            along = jnp.mean(g * mixed, axis=-1, keepdims=True) * inverse
            normed = mixed * inverse
            grad = (inverse * (g - normed * along)).astype(BF16)
            grad_ref[:, head(h)] = grad
            for ref in state_refs:
                ref[head(h), :] = dot_nn(qt_ref[cols, :], grad).astype(BF16)
            normed_ref[:, head(h)] = normed.astype(BF16)


def mid(half_of, roles, me, shared, token, earlier, keep=(), other=()):
    merge = len(other) - len(keep)
    length, width = shared[0].shape
    half_shape = jax.ShapeDtypeStruct((length, width // 2), BF16)
    state_shape = jax.ShapeDtypeStruct(earlier[0].shape, BF16)
    normed, grad, low, token, *states_out = pl.pallas_call(
        functools.partial(mid_kernel, half_of, roles, keep, merge),
        in_specs=[SMEM_SPEC] + [VMEM_SPEC] * (5 + len(other) + len(earlier)),
        out_specs=(VMEM_SPEC,) * (5 + merge),
        **params("mid", (half_shape, half_shape, state_shape, TOKEN) + (state_shape,) * (1 + merge)),
    )(me, *shared, token, *other, *earlier)
    return (normed, grad, low), *states_out, token


def back_kernel(half_of, roles, sets, me_ref, q_ref, k_ref, v_ref, token_ref, *refs):
    normed_ref, gq_ref, gk_ref, gv_ref, done_ref, gq_buf, n_buf, gq_sem, n_sem = refs[-9:]
    length = q_ref.shape[0]
    rows = lax.broadcasted_iota(jnp.int32, (length, length), 0)
    columns = lax.broadcasted_iota(jnp.int32, (length, length), 1)
    mask, mask_t = columns <= rows, rows <= columns
    heads = gk_ref.shape[1] // DH
    half = half_of(me_ref[0])

    def chosen(index, place):
        value = refs[index][place]
        if sets > 1:
            value = jnp.where(among(me_ref[0], roles), refs[3 + index][place], value)
        return value

    copies = []
    for h in range(heads):
        cols = half_columns(half, h, heads)
        n_buf[h] = chosen(0, (slice(None), head(h)))
        copies.append(pltpu.make_async_copy(n_buf.at[h], normed_ref.at[:, cols], n_sem.at[h]))
        copies[-1].start()
        q, k, v = (ref[:, cols] for ref in (q_ref, k_ref, v_ref))
        grad = chosen(1, (slice(None), head(h)))
        earlier = chosen(2, (head(h), slice(None)))
        scores_t = jnp.where(mask_t, dot_nt(k, q), 0.0).astype(BF16)
        grad_scores = jnp.where(mask, dot_nt(grad, v), 0.0).astype(BF16)
        grad_scores_t = jnp.where(mask_t, dot_nt(v, grad), 0.0).astype(BF16)
        gq_buf[h] = (dot_nn(grad_scores, k) + dot_nt(grad, earlier)).astype(BF16)
        copies.append(pltpu.make_async_copy(gq_buf.at[h], gq_ref.at[:, cols], gq_sem.at[h]))
        copies[-1].start()
        gk_ref[:, head(h)] = dot_nn(grad_scores_t, q)
        gv_ref[:, head(h)] = dot_nn(scores_t, grad)
    done_ref[...] = token_ref[...]
    for copy in copies:
        copy.wait()


def back(half_of, roles, me, q, k, v, token, sets, filled=()):
    length, width = q.shape
    heads = width // (2 * DH)
    whole = jax.ShapeDtypeStruct(q.shape, BF16)
    half_shape = jax.ShapeDtypeStruct((length, width // 2), F32)
    first = 5 + 3 * len(sets)
    buffers = pltpu.VMEM((heads, length, DH), BF16)
    return pl.pallas_call(
        functools.partial(back_kernel, half_of, roles, len(sets)),
        in_specs=[SMEM_SPEC] + [VMEM_SPEC] * (first - 1) + [HBM_SPEC] * len(filled),
        out_specs=(HBM_SPEC, HBM_SPEC, VMEM_SPEC, VMEM_SPEC, VMEM_SPEC),
        scratch_shapes=[buffers, buffers] + [pltpu.SemaphoreType.DMA((heads,))] * 2,
        input_output_aliases={first: 0, first + 1: 1} if filled else {},
        **params("back", (whole, whole, half_shape, half_shape, TOKEN)),
    )(me, q, k, v, token, *(x for one in sets for x in one), *filled)


def post_kernel(half_of, parts, me_ref, k_ref, v_ref, gk_in_ref, gv_in_ref, token_ref, *refs):
    l_refs, (gk_ref, gv_ref, done_ref, gk_buf, gv_buf, gk_sem, gv_sem) = refs[:parts], refs[-7:]
    done_ref[...] = token_ref[...]
    heads = gk_in_ref.shape[1] // DH
    half = half_of(me_ref[0])
    copies = []
    for h in range(heads):
        cols = half_columns(half, h, heads)
        later = total(l_refs, head(h))
        gk_buf[h] = (gk_in_ref[:, head(h)] + dot_nt(v_ref[:, cols], later)).astype(BF16)
        copies.append(pltpu.make_async_copy(gk_buf.at[h], gk_ref.at[:, cols], gk_sem.at[h]))
        copies[-1].start()
        gv_buf[h] = (gv_in_ref[:, head(h)] + dot_nn(k_ref[:, cols], later)).astype(BF16)
        copies.append(pltpu.make_async_copy(gv_buf.at[h], gv_ref.at[:, cols], gv_sem.at[h]))
        copies[-1].start()
    for copy in copies:
        copy.wait()


def post(half_of, me, k, v, gk_in, gv_in, token, later, filled=()):
    length, width = k.shape
    heads = width // (2 * DH)
    first = 6 + len(later)
    return pl.pallas_call(
        functools.partial(post_kernel, half_of, len(later)),
        in_specs=[SMEM_SPEC] + [VMEM_SPEC] * (first - 1) + [HBM_SPEC] * len(filled),
        out_specs=(HBM_SPEC, HBM_SPEC, VMEM_SPEC),
        scratch_shapes=[pltpu.VMEM((heads, length, DH), BF16)] * 2 + [pltpu.SemaphoreType.DMA((heads,))] * 2,
        input_output_aliases={first: 0, first + 1: 1} if filled else {},
        **params("post", (jax.ShapeDtypeStruct(k.shape, BF16), jax.ShapeDtypeStruct(k.shape, BF16), TOKEN)),
    )(me, k, v, gk_in, gv_in, token, *later, *filled)


def even_half(me):
    return 1 - lax.rem(me, 2)


def odd_half(me):
    return lax.rem(me, 2)


def rows_of(array):
    return array.reshape(array.shape[1:])


def shards_four(queries, key_vectors, value_vectors, grad_output):
    out_shape = queries.shape
    q, k, v, g = (rows_of(x) for x in (queries, key_vectors, value_vectors, grad_output))
    me = lax.axis_index("ctx").astype(jnp.int32).reshape(1)
    token = jnp.zeros(TOKEN.shape, TOKEN.dtype)

    def send(x, pairs):
        return lax.ppermute(x, "ctx", pairs)

    s_a, token = states((((0,), ((0, 0),)),), me, k, v, token)
    r_a = send(s_a, [(0, 1)])
    s_x, s_b, token = states((((0,), ((1, 0),)), ((1,), ((1, 1), (0, 0)))), me, k, v, token)
    r_b = send(s_b, [(1, 2)])
    s_c, s_y, token = states((((2,), ((0, 0), (1, 1))),), me, k, v, token, (0, 0), (s_x,))
    r_c = send(s_c, [(0, 2), (2, 3)])
    intra_out, qt, token = intra(q, k, v, token)
    shared = (q, qt, g, intra_out)
    s12, token = add(token, r_a, s_x)
    r_far = send(s12, [(1, 3)])
    r_near = send(s12, [(0, 1), (1, 2)])
    s123, token = add(token, r_b, r_c, s_y)
    first, g_first, token = mid(even_half, (0, 1, 2), me, shared, token, (r_a, r_b, r_c))
    r_last = send(s123, [(2, 3)])
    first_end, g_one, token = mid(even_half, (3,), me, shared, token, (r_c, r_far), (2,), (g_first,))
    u_one = send(g_one, [(3, 2), (2, 1)])
    second, g_rest, token = mid(odd_half, (0, 1, 2), me, shared, token, (r_near,))
    second_end, g_two, g_second, token = mid(odd_half, (3,), me, shared, token, (r_last,), (1,), (g_first, g_rest))
    u_two = send(g_two, [(3, 1), (1, 0)])
    normed, grad_q, gk_second, gv_second, token = back(odd_half, (3,), me, q, k, v, token, (second, second_end))
    g12, token = add(token, u_one, g_second)
    w_far = send(g12, [(2, 0)])
    w_near = send(g12, [(3, 2), (2, 1)])
    g123, token = add(token, u_one, u_two, g_second)
    w_last = send(g123, [(1, 0)])
    normed, grad_q, gk_first, gv_first, token = back(
        even_half, (3,), me, q, k, v, token, (first, first_end), (normed, grad_q)
    )
    *filled, token = post(odd_half, me, k, v, gk_second, gv_second, token, (u_one, u_two, w_far))
    l_near, token = add(token, w_near)
    grad_k, grad_v, token = post(even_half, me, k, v, gk_first, gv_first, token, (l_near, w_last), filled)
    return tuple(x.reshape(out_shape) for x in (normed, grad_q, grad_k, grad_v))


def scan_states(first, second, count, backward):
    rows = first.shape[0] * 2
    shares = jnp.concatenate([first, second], axis=0).reshape(count, rows // count, DH)
    shares = lax.all_to_all(shares, "ctx", split_axis=0, concat_axis=0, tiled=True).astype(F32)
    running = jnp.cumsum(shares, axis=0)
    sums = running[-1:] - running if backward else running - shares
    sums = lax.all_to_all(sums.astype(BF16), "ctx", split_axis=0, concat_axis=0, tiled=True)
    sums = sums.reshape(rows, DH)
    return sums[: rows // 2], sums[rows // 2 :]


def low_half(me):
    return 0


def high_half(me):
    return 1


def shards_any(count, queries, key_vectors, value_vectors, grad_output):
    out_shape = queries.shape
    q, k, v, g = (rows_of(x) for x in (queries, key_vectors, value_vectors, grad_output))
    me = lax.axis_index("ctx").astype(jnp.int32).reshape(1)
    token = jnp.zeros(TOKEN.shape, TOKEN.dtype)
    s1, s2, token = states((((), ((0, 0), (1, 1))),), me, k, v, token)
    e1, e2 = scan_states(s1, s2, count, False)
    intra_out, qt, token = intra(q, k, v, token)
    shared = (q, qt, g, intra_out)
    low, g1, token = mid(low_half, (), me, shared, token, (e1,))
    high, g2, token = mid(high_half, (), me, shared, token, (e2,))
    l1, l2 = scan_states(g1, g2, count, True)
    normed, grad_q, gk1, gv1, token = back(low_half, (), me, q, k, v, token, (low,))
    normed, grad_q, gk2, gv2, token = back(high_half, (), me, q, k, v, token, (high,), (normed, grad_q))
    *filled, token = post(low_half, me, k, v, gk1, gv1, token, (l1,))
    grad_k, grad_v, token = post(high_half, me, k, v, gk2, gv2, token, (l2,), filled)
    return tuple(x.reshape(out_shape) for x in (normed, grad_q, grad_k, grad_v))


def solution(mesh):
    placed = P(("groups", "dp"), "ctx", "tp")
    count = mesh.shape["ctx"]

    def shards(*args):
        if count == 4:
            return shards_four(*args)
        return shards_any(count, *args)

    return jax.shard_map(
        shards,
        mesh=mesh,
        in_specs=(placed,) * 4,
        out_specs=(placed,) * 4,
        check_vma=False,
    )
```

```python
import functools

import jax
import jax.numpy as jnp
from jax import lax
from jax.experimental import pallas as pl
from jax.experimental.pallas import tpu as pltpu
from jax.sharding import PartitionSpec as P

DH = 128
norm_eps = 1e-06
F32 = jnp.float32
BF16 = jnp.bfloat16

VMEM_SPEC = pl.BlockSpec(memory_space=pltpu.VMEM)
HBM_SPEC = pl.BlockSpec(memory_space=pltpu.HBM)
SMEM_SPEC = pl.BlockSpec(memory_space=pltpu.SMEM)
COST = pl.CostEstimate(flops=0, transcendentals=0, bytes_accessed=4096)
PARAMS = pltpu.CompilerParams(vmem_limit_bytes=16 << 20)


def params(name, parts):
    return dict(compiler_params=PARAMS, cost_estimate=COST, name=name, out_shape=parts)


def dot_nn(a, b):
    return lax.dot_general(a, b, (((1,), (0,)), ((), ())), preferred_element_type=F32)


def dot_nt(a, b):
    return lax.dot_general(a, b, (((1,), (1,)), ((), ())), preferred_element_type=F32)


def dot_tn(a, b):
    return lax.dot_general(a, b, (((0,), (0,)), ((), ())), preferred_element_type=F32)


def head(index):
    return slice(index * DH, (index + 1) * DH)


def causal(length):
    rows = lax.broadcasted_iota(jnp.int32, (length, length), 0)
    columns = lax.broadcasted_iota(jnp.int32, (length, length), 1)
    return columns <= rows


def half_columns(half, h, heads):
    return pl.ds(pl.multiple_of((half * heads + h) * DH, DH), DH)


def among(me, roles):
    hit = me == roles[0]
    for role in roles[1:]:
        hit = hit | (me == role)
    return hit


def on(me, roles):
    return pl.when(among(me, roles)) if roles else lambda body: body()


def near_state_kernel(half, roles, keep, me_ref, k_ref, v_ref, token_ref, *refs):
    passed = (len(refs) - 2 - len(keep)) // 2
    out_ref, done_ref, *copies = refs[-2 - passed :]
    heads = out_ref.shape[0] // DH
    done_ref[...] = token_ref[...]
    for source, copy in zip(refs[len(keep) :], copies):
        copy[...] = source[...]
    if keep:

        @on(me_ref[0], keep)
        def _():
            out_ref[...] = refs[0][...]

    @on(me_ref[0], roles)
    def _():
        for h in range(heads):
            cols = head(half * heads + h)
            out_ref[head(h), :] = dot_tn(k_ref[:, cols], v_ref[:, cols]).astype(BF16)


def near_states(half, roles, me, k, v, token, keep=(), spare=(), passed=()):
    shape = jax.ShapeDtypeStruct((k.shape[1] // 2, DH), BF16)
    return pl.pallas_call(
        functools.partial(near_state_kernel, half, roles, keep),
        in_specs=[SMEM_SPEC] + [VMEM_SPEC] * (3 + len(spare) + len(passed)),
        out_specs=(VMEM_SPEC,) * (2 + len(passed)),
        **params("near_states", (shape, TOKEN) + (shape,) * len(passed)),
    )(me, k, v, token, *spare, *passed)


def state_kernel(plan, me_ref, k_ref, v_ref, token_ref, *refs):
    outs, (done_ref, k_buf, v_buf, k_sem, v_sem) = refs[:-5], refs[-5:]
    heads = outs[0].shape[0] // DH
    done_ref[...] = token_ref[...]
    for roles, pieces in plan:

        @on(me_ref[0], roles)
        def _():
            copies = []
            for half, out in pieces:
                for h in range(heads):
                    cols, slot = head(half * heads + h), len(copies)
                    pair = (
                        pltpu.make_async_copy(k_ref.at[:, cols], k_buf.at[slot], k_sem.at[slot]),
                        pltpu.make_async_copy(v_ref.at[:, cols], v_buf.at[slot], v_sem.at[slot]),
                    )
                    for copy in pair:
                        copy.start()
                    copies.append((outs[out], head(h), pair))
            for slot, (out_ref, rows, pair) in enumerate(copies):
                for copy in pair:
                    copy.wait()
                out_ref[rows, :] = dot_tn(k_buf[slot], v_buf[slot]).astype(BF16)


def states(plan, me, k, v, token):
    length, width = k.shape
    count = 1 + max(out for _, pieces in plan for _, out in pieces)
    slots = max(len(pieces) for _, pieces in plan) * width // (2 * DH)
    k, v = (pltpu.with_memory_space_constraint(x, pltpu.HBM) for x in (k, v))
    shape = jax.ShapeDtypeStruct((width // 2, DH), BF16)
    return pl.pallas_call(
        functools.partial(state_kernel, plan),
        in_specs=[SMEM_SPEC, HBM_SPEC, HBM_SPEC, VMEM_SPEC],
        out_specs=(VMEM_SPEC,) * (count + 1),
        scratch_shapes=[pltpu.VMEM((slots, length, DH), BF16)] * 2 + [pltpu.SemaphoreType.DMA((slots,))] * 2,
        **params("states", (shape,) * count + (TOKEN,)),
    )(me, k, v, token)


TOKEN = jax.ShapeDtypeStruct((8, DH), F32)


def intra_kernel(q_ref, k_ref, v_ref, token_ref, out_ref, qt_ref, done_ref):
    mask = causal(q_ref.shape[0])
    for h in range(q_ref.shape[1] // DH):
        q = q_ref[:, head(h)]
        scores = jnp.where(mask, dot_nt(q, k_ref[:, head(h)]), 0.0).astype(BF16)
        out_ref[:, head(h)] = dot_nn(scores, v_ref[:, head(h)])
        qt_ref[head(h), :] = q.T
    done_ref[...] = token_ref[...]


def intra(q, k, v, token):
    length, width = q.shape
    return pl.pallas_call(
        intra_kernel,
        in_specs=[VMEM_SPEC] * 4,
        out_specs=(VMEM_SPEC,) * 3,
        **params("intra", (jax.ShapeDtypeStruct(q.shape, F32), jax.ShapeDtypeStruct((width, length), BF16), TOKEN)),
    )(q, k, v, token)


def total(refs, rows=slice(None)):
    value = refs[0][rows, :].astype(F32)
    for ref in refs[1:]:
        value = value + ref[rows, :].astype(F32)
    return value.astype(BF16)


def add_kernel(token_ref, *refs):
    refs[-2][...] = total(refs[:-2])
    refs[-1][...] = token_ref[...]


def add(token, *arrays):
    return pl.pallas_call(
        add_kernel,
        in_specs=[VMEM_SPEC] * (1 + len(arrays)),
        out_specs=(VMEM_SPEC,) * 2,
        **params("add", (jax.ShapeDtypeStruct(arrays[0].shape, BF16), TOKEN)),
    )(token, *arrays)


def half_columns(half, h, heads):
    return pl.ds(pl.multiple_of((half * heads + h) * DH, DH), DH)


def mid_kernel(half_of, roles, keep, merge, me_ref, q_ref, qt_ref, g_ref, intra_ref, token_ref, *refs):
    normed_ref, grad_ref, earlier_ref, done_ref, *state_refs = refs[-5 - merge :]
    other, e_refs = refs[: len(keep) + merge], refs[len(keep) + merge : -5 - merge]
    state_ref = state_refs[0]
    heads = state_ref.shape[0] // DH
    done_ref[...] = token_ref[...]
    if keep:

        @on(me_ref[0], keep)
        def _():
            state_ref[...] = other[0][...]

    if merge:

        @pl.when(jnp.logical_not(among(me_ref[0], roles)))
        def _():
            state_refs[1][...] = other[-1][...]

    @on(me_ref[0], roles)
    def _():
        half = half_of(me_ref[0])
        for h in range(heads):
            cols = half_columns(half, h, heads)
            earlier = total(e_refs, head(h))
            earlier_ref[head(h), :] = earlier
            mixed = intra_ref[:, cols] + dot_nn(q_ref[:, cols], earlier)
            g = g_ref[:, cols].astype(F32)
            inverse = lax.rsqrt(jnp.mean(mixed * mixed, axis=-1, keepdims=True) + norm_eps)
            along = jnp.mean(g * mixed, axis=-1, keepdims=True) * inverse
            normed = mixed * inverse
            grad = (inverse * (g - normed * along)).astype(BF16)
            grad_ref[:, head(h)] = grad
            state = dot_nn(qt_ref[cols, :], grad).astype(BF16)
            for ref in state_refs:
                ref[head(h), :] = state
            normed_ref[:, head(h)] = normed.astype(BF16)


def mid(half_of, roles, me, shared, token, earlier, keep=(), other=()):
    merge = len(other) - len(keep)
    length, width = shared[0].shape
    half_shape = jax.ShapeDtypeStruct((length, width // 2), BF16)
    state_shape = jax.ShapeDtypeStruct(earlier[0].shape, BF16)
    normed, grad, low, token, *states_out = pl.pallas_call(
        functools.partial(mid_kernel, half_of, roles, keep, merge),
        in_specs=[SMEM_SPEC] + [VMEM_SPEC] * (5 + len(other) + len(earlier)),
        out_specs=(VMEM_SPEC,) * (5 + merge),
        **params("mid", (half_shape, half_shape, state_shape, TOKEN) + (state_shape,) * (1 + merge)),
    )(me, *shared, token, *other, *earlier)
    return (normed, grad, low), *states_out, token


def back_kernel(half_of, roles, sets, me_ref, q_ref, k_ref, v_ref, token_ref, *refs):
    normed_ref, gq_ref, gk_ref, gv_ref, done_ref, gq_buf, n_buf, gq_sem, n_sem = refs[-9:]
    length = q_ref.shape[0]
    rows = lax.broadcasted_iota(jnp.int32, (length, length), 0)
    columns = lax.broadcasted_iota(jnp.int32, (length, length), 1)
    mask, mask_t = columns <= rows, rows <= columns
    heads = gk_ref.shape[1] // DH
    half = half_of(me_ref[0])

    def chosen(index, place):
        value = refs[index][place]
        if sets > 1:
            value = jnp.where(among(me_ref[0], roles), refs[3 + index][place], value)
        return value

    copies = []
    for h in range(heads):
        cols = half_columns(half, h, heads)
        n_buf[h] = chosen(0, (slice(None), head(h)))
        copies.append(pltpu.make_async_copy(n_buf.at[h], normed_ref.at[:, cols], n_sem.at[h]))
        copies[-1].start()
        q, k, v = (ref[:, cols] for ref in (q_ref, k_ref, v_ref))
        grad = chosen(1, (slice(None), head(h)))
        earlier = chosen(2, (head(h), slice(None)))
        scores_t = jnp.where(mask_t, dot_nt(k, q), 0.0).astype(BF16)
        grad_scores = jnp.where(mask, dot_nt(grad, v), 0.0).astype(BF16)
        grad_scores_t = jnp.where(mask_t, dot_nt(v, grad), 0.0).astype(BF16)
        gq_buf[h] = (dot_nn(grad_scores, k) + dot_nt(grad, earlier)).astype(BF16)
        copies.append(pltpu.make_async_copy(gq_buf.at[h], gq_ref.at[:, cols], gq_sem.at[h]))
        copies[-1].start()
        gk_ref[:, head(h)] = dot_nn(grad_scores_t, q)
        gv_ref[:, head(h)] = dot_nn(scores_t, grad)
    done_ref[...] = token_ref[...]
    for copy in copies:
        copy.wait()


def back(half_of, roles, me, q, k, v, token, sets, filled=()):
    length, width = q.shape
    heads = width // (2 * DH)
    whole = jax.ShapeDtypeStruct(q.shape, BF16)
    half_shape = jax.ShapeDtypeStruct((length, width // 2), F32)
    first = 5 + 3 * len(sets)
    buffers = pltpu.VMEM((heads, length, DH), BF16)
    return pl.pallas_call(
        functools.partial(back_kernel, half_of, roles, len(sets)),
        in_specs=[SMEM_SPEC] + [VMEM_SPEC] * (first - 1) + [HBM_SPEC] * len(filled),
        out_specs=(HBM_SPEC, HBM_SPEC, VMEM_SPEC, VMEM_SPEC, VMEM_SPEC),
        scratch_shapes=[buffers, buffers] + [pltpu.SemaphoreType.DMA((heads,))] * 2,
        input_output_aliases={first: 0, first + 1: 1} if filled else {},
        **params("back", (whole, whole, half_shape, half_shape, TOKEN)),
    )(me, q, k, v, token, *(x for one in sets for x in one), *filled)


def post_first_kernel(half_of, parts, *refs):
    refs[-5][...] = refs[5][...]
    post_kernel(half_of, parts, *refs[:-5], *refs[-4:])


def post_kernel(half_of, parts, me_ref, k_ref, v_ref, gk_in_ref, gv_in_ref, token_ref, *refs):
    l_refs, (gk_ref, gv_ref, gk_buf, gv_buf, gk_sem, gv_sem) = refs[:parts], refs[-6:]
    heads = gk_in_ref.shape[1] // DH
    half = half_of(me_ref[0])
    copies = []
    for h in range(heads):
        cols = half_columns(half, h, heads)
        later = total(l_refs, head(h))
        gk_buf[h] = (gk_in_ref[:, head(h)] + dot_nt(v_ref[:, cols], later)).astype(BF16)
        copies.append(pltpu.make_async_copy(gk_buf.at[h], gk_ref.at[:, cols], gk_sem.at[h]))
        copies[-1].start()
        gv_buf[h] = (gv_in_ref[:, head(h)] + dot_nn(k_ref[:, cols], later)).astype(BF16)
        copies.append(pltpu.make_async_copy(gv_buf.at[h], gv_ref.at[:, cols], gv_sem.at[h]))
        copies[-1].start()
    for copy in copies:
        copy.wait()


def post(half_of, me, k, v, gk_in, gv_in, token, later, filled=()):
    length, width = k.shape
    heads = width // (2 * DH)
    first = 6 + len(later)
    whole = jax.ShapeDtypeStruct(k.shape, BF16)
    return pl.pallas_call(
        functools.partial(post_kernel if filled else post_first_kernel, half_of, len(later)),
        in_specs=[SMEM_SPEC] + [VMEM_SPEC] * (first - 1) + [HBM_SPEC] * len(filled),
        out_specs=(HBM_SPEC, HBM_SPEC) if filled else (HBM_SPEC, HBM_SPEC, VMEM_SPEC),
        scratch_shapes=[pltpu.VMEM((heads, length, DH), BF16)] * 2 + [pltpu.SemaphoreType.DMA((heads,))] * 2,
        input_output_aliases={first: 0, first + 1: 1} if filled else {},
        **params("post", (whole, whole) if filled else (whole, whole, TOKEN)),
    )(me, k, v, gk_in, gv_in, token, *later, *filled)


def even_half(me):
    return 1 - lax.rem(me, 2)


def odd_half(me):
    return lax.rem(me, 2)


def rows_of(array):
    return array.reshape(array.shape[1:])


def shards_four(queries, key_vectors, value_vectors, grad_output):
    out_shape = queries.shape
    q, k, v, g = (rows_of(x) for x in (queries, key_vectors, value_vectors, grad_output))
    me = lax.axis_index("ctx").astype(jnp.int32).reshape(1)
    token = jnp.zeros(TOKEN.shape, TOKEN.dtype)

    def send(x, pairs):
        return lax.ppermute(x, "ctx", pairs)

    s_a, token = states((((0,), ((0, 0),)),), me, k, v, token)
    r_a = send(s_a, [(0, 1)])
    s_b, token = near_states(1, (0, 1), me, k, v, token)
    r_b = send(s_b, [(1, 2)])
    s_c, token = near_states(0, (1, 2), me, k, v, token, (0,), (s_b,))
    r_c = send(s_c, [(0, 2), (2, 3)])
    intra_out, qt, token = intra(q, k, v, token)
    shared = (q, qt, g, intra_out)
    s12, token = add(token, r_a, s_c)
    r_far = send(s12, [(1, 3)])
    s_y, token, s12 = near_states(1, (2,), me, k, v, token, passed=(s12,))
    r_near = send(s12, [(0, 1), (1, 2)])
    r_b, token = add(token, r_b)
    s123, token = add(token, r_b, r_c, s_y)
    first, g_first, token = mid(even_half, (0, 1, 2), me, shared, token, (r_a, r_b, r_c))
    r_last = send(s123, [(2, 3)])
    first_end, g_one, token = mid(even_half, (3,), me, shared, token, (r_c, r_far), (2,), (g_first,))
    u_one = send(g_one, [(3, 2), (2, 1)])
    second, g_rest, token = mid(odd_half, (0, 1, 2), me, shared, token, (r_near,))
    second_end, g_two, g_second, token = mid(odd_half, (3,), me, shared, token, (r_last,), (1,), (g_first, g_rest))
    u_two = send(g_two, [(3, 1), (1, 0)])
    normed, grad_q, gk_second, gv_second, token = back(odd_half, (3,), me, q, k, v, token, (second, second_end))
    g12, token = add(token, u_one, g_second)
    w_far = send(g12, [(2, 0)])
    w_near = send(g12, [(3, 2), (2, 1)])
    g123, token = add(token, u_one, u_two, g_second)
    w_last = send(g123, [(1, 0)])
    normed, grad_q, gk_first, gv_first, token = back(
        even_half, (3,), me, q, k, v, token, (first, first_end), (normed, grad_q)
    )
    *filled, token = post(odd_half, me, k, v, gk_second, gv_second, token, (u_one, u_two, w_far))
    l_near, token = add(token, w_near)
    grad_k, grad_v = post(even_half, me, k, v, gk_first, gv_first, token, (l_near, w_last), filled)
    return tuple(x.reshape(out_shape) for x in (normed, grad_q, grad_k, grad_v))


def scan_states(first, second, count, backward):
    rows = first.shape[0] * 2
    shares = jnp.concatenate([first, second], axis=0).reshape(count, rows // count, DH)
    shares = lax.all_to_all(shares, "ctx", split_axis=0, concat_axis=0, tiled=True).astype(F32)
    running = jnp.cumsum(shares, axis=0)
    sums = running[-1:] - running if backward else running - shares
    sums = lax.all_to_all(sums.astype(BF16), "ctx", split_axis=0, concat_axis=0, tiled=True)
    sums = sums.reshape(rows, DH)
    return sums[: rows // 2], sums[rows // 2 :]


def low_half(me):
    return 0


def high_half(me):
    return 1


def shards_any(count, queries, key_vectors, value_vectors, grad_output):
    out_shape = queries.shape
    q, k, v, g = (rows_of(x) for x in (queries, key_vectors, value_vectors, grad_output))
    me = lax.axis_index("ctx").astype(jnp.int32).reshape(1)
    token = jnp.zeros(TOKEN.shape, TOKEN.dtype)
    s1, s2, token = states((((), ((0, 0), (1, 1))),), me, k, v, token)
    e1, e2 = scan_states(s1, s2, count, False)
    intra_out, qt, token = intra(q, k, v, token)
    shared = (q, qt, g, intra_out)
    low, g1, token = mid(low_half, (), me, shared, token, (e1,))
    high, g2, token = mid(high_half, (), me, shared, token, (e2,))
    l1, l2 = scan_states(g1, g2, count, True)
    normed, grad_q, gk1, gv1, token = back(low_half, (), me, q, k, v, token, (low,))
    normed, grad_q, gk2, gv2, token = back(high_half, (), me, q, k, v, token, (high,), (normed, grad_q))
    *filled, token = post(low_half, me, k, v, gk1, gv1, token, (l1,))
    grad_k, grad_v = post(high_half, me, k, v, gk2, gv2, token, (l2,), filled)
    return tuple(x.reshape(out_shape) for x in (normed, grad_q, grad_k, grad_v))


def solution(mesh):
    placed = P(("groups", "dp"), "ctx", "tp")
    count = mesh.shape["ctx"]

    def shards(*args):
        if count == 4:
            return shards_four(*args)
        return shards_any(count, *args)

    return jax.shard_map(
        shards,
        mesh=mesh,
        in_specs=(placed,) * 4,
        out_specs=(placed,) * 4,
        check_vma=False,
    )
```

```python
import functools

import jax
import jax.numpy as jnp
from jax import lax
from jax.experimental import pallas as pl
from jax.experimental.pallas import tpu as pltpu
from jax.sharding import PartitionSpec as P

DH = 128
norm_eps = 1e-06
F32 = jnp.float32
BF16 = jnp.bfloat16

VMEM_SPEC = pl.BlockSpec(memory_space=pltpu.VMEM)
HBM_SPEC = pl.BlockSpec(memory_space=pltpu.HBM)
SMEM_SPEC = pl.BlockSpec(memory_space=pltpu.SMEM)
COST = pl.CostEstimate(flops=0, transcendentals=0, bytes_accessed=4096)
PARAMS = pltpu.CompilerParams(vmem_limit_bytes=16 << 20)


def params(name, parts):
    return dict(compiler_params=PARAMS, cost_estimate=COST, name=name, out_shape=parts)


def dot_nn(a, b):
    return lax.dot_general(a, b, (((1,), (0,)), ((), ())), preferred_element_type=F32)


def dot_nt(a, b):
    return lax.dot_general(a, b, (((1,), (1,)), ((), ())), preferred_element_type=F32)


def dot_tn(a, b):
    return lax.dot_general(a, b, (((0,), (0,)), ((), ())), preferred_element_type=F32)


def head(index):
    return slice(index * DH, (index + 1) * DH)


def causal(length):
    rows = lax.broadcasted_iota(jnp.int32, (length, length), 0)
    columns = lax.broadcasted_iota(jnp.int32, (length, length), 1)
    return columns <= rows


def half_columns(half, h, heads):
    return pl.ds(pl.multiple_of((half * heads + h) * DH, DH), DH)


def among(me, roles):
    hit = me == roles[0]
    for role in roles[1:]:
        hit = hit | (me == role)
    return hit


def on(me, roles):
    return pl.when(among(me, roles)) if roles else lambda body: body()


def near_state_kernel(half, roles, keep, me_ref, k_ref, v_ref, token_ref, *refs):
    passed = (len(refs) - 2 - len(keep)) // 2
    out_ref, done_ref, *copies = refs[-2 - passed :]
    heads = out_ref.shape[0] // DH
    done_ref[...] = token_ref[...]
    for source, copy in zip(refs[len(keep) :], copies):
        copy[...] = source[...]
    if keep:

        @on(me_ref[0], keep)
        def _():
            out_ref[...] = refs[0][...]

    @on(me_ref[0], roles)
    def _():
        for h in range(heads):
            cols = head(half * heads + h)
            out_ref[head(h), :] = dot_tn(k_ref[:, cols], v_ref[:, cols]).astype(BF16)


def near_states(half, roles, me, k, v, token, keep=(), spare=(), passed=()):
    shape = jax.ShapeDtypeStruct((k.shape[1] // 2, DH), BF16)
    return pl.pallas_call(
        functools.partial(near_state_kernel, half, roles, keep),
        in_specs=[SMEM_SPEC] + [VMEM_SPEC] * (3 + len(spare) + len(passed)),
        out_specs=(VMEM_SPEC,) * (2 + len(passed)),
        **params("near_states", (shape, TOKEN) + (shape,) * len(passed)),
    )(me, k, v, token, *spare, *passed)


def state_kernel(plan, me_ref, k_ref, v_ref, token_ref, *refs):
    outs, (done_ref, k_buf, v_buf, k_sem, v_sem) = refs[:-5], refs[-5:]
    heads = outs[0].shape[0] // DH
    done_ref[...] = token_ref[...]
    for roles, pieces in plan:

        @on(me_ref[0], roles)
        def _():
            copies = []
            for half, out in pieces:
                for h in range(heads):
                    cols, slot = head(half * heads + h), len(copies)
                    pair = (
                        pltpu.make_async_copy(k_ref.at[:, cols], k_buf.at[slot], k_sem.at[slot]),
                        pltpu.make_async_copy(v_ref.at[:, cols], v_buf.at[slot], v_sem.at[slot]),
                    )
                    for copy in pair:
                        copy.start()
                    copies.append((outs[out], head(h), pair))
            for slot, (out_ref, rows, pair) in enumerate(copies):
                for copy in pair:
                    copy.wait()
                out_ref[rows, :] = dot_tn(k_buf[slot], v_buf[slot]).astype(BF16)


def states(plan, me, k, v, token):
    length, width = k.shape
    count = 1 + max(out for _, pieces in plan for _, out in pieces)
    slots = max(len(pieces) for _, pieces in plan) * width // (2 * DH)
    k, v = (pltpu.with_memory_space_constraint(x, pltpu.HBM) for x in (k, v))
    shape = jax.ShapeDtypeStruct((width // 2, DH), BF16)
    return pl.pallas_call(
        functools.partial(state_kernel, plan),
        in_specs=[SMEM_SPEC, HBM_SPEC, HBM_SPEC, VMEM_SPEC],
        out_specs=(VMEM_SPEC,) * (count + 1),
        scratch_shapes=[pltpu.VMEM((slots, length, DH), BF16)] * 2 + [pltpu.SemaphoreType.DMA((slots,))] * 2,
        **params("states", (shape,) * count + (TOKEN,)),
    )(me, k, v, token)


TOKEN = jax.ShapeDtypeStruct((8, DH), F32)


def intra_kernel(q_ref, k_ref, v_ref, token_ref, out_ref, qt_ref, done_ref):
    mask = causal(q_ref.shape[0])
    heads = q_ref.shape[1] // DH

    def scores_of(h):
        return jnp.where(mask, dot_nt(q_ref[:, head(h)], k_ref[:, head(h)]), 0.0).astype(BF16)

    scores = scores_of(0)
    for h in range(heads):
        ahead = scores_of(h + 1) if h + 1 < heads else None
        out_ref[:, head(h)] = dot_nn(scores, v_ref[:, head(h)])
        qt_ref[head(h), :] = q_ref[:, head(h)].T
        scores = ahead
    done_ref[...] = token_ref[...]


def intra(q, k, v, token):
    length, width = q.shape
    return pl.pallas_call(
        intra_kernel,
        in_specs=[VMEM_SPEC] * 4,
        out_specs=(VMEM_SPEC,) * 3,
        **params("intra", (jax.ShapeDtypeStruct(q.shape, F32), jax.ShapeDtypeStruct((width, length), BF16), TOKEN)),
    )(q, k, v, token)


def total(refs, rows=slice(None)):
    value = refs[0][rows, :].astype(F32)
    for ref in refs[1:]:
        value = value + ref[rows, :].astype(F32)
    return value.astype(BF16)


def add_kernel(token_ref, *refs):
    refs[-2][...] = total(refs[:-2])
    refs[-1][...] = token_ref[...]


def add(token, *arrays):
    return pl.pallas_call(
        add_kernel,
        in_specs=[VMEM_SPEC] * (1 + len(arrays)),
        out_specs=(VMEM_SPEC,) * 2,
        **params("add", (jax.ShapeDtypeStruct(arrays[0].shape, BF16), TOKEN)),
    )(token, *arrays)


def half_columns(half, h, heads):
    return pl.ds(pl.multiple_of((half * heads + h) * DH, DH), DH)


def half_copy(half, buf, ref, sem):
    width = buf.shape[1]
    return pltpu.make_async_copy(buf, ref.at[:, pl.ds(pl.multiple_of(half * width, width), width)], sem)


def mid_kernel(half_of, roles, keep, merge, me_ref, q_ref, qt_ref, g_ref, intra_ref, token_ref, *refs):
    normed_ref, grad_ref, earlier_ref, done_ref, *state_refs = refs[-5 - merge :]
    other, e_refs = refs[: len(keep) + merge], refs[len(keep) + merge : -5 - merge]
    state_ref = state_refs[0]
    heads = state_ref.shape[0] // DH
    done_ref[...] = token_ref[...]
    if keep:

        @on(me_ref[0], keep)
        def _():
            state_ref[...] = other[0][...]

    if merge:

        @pl.when(jnp.logical_not(among(me_ref[0], roles)))
        def _():
            state_refs[1][...] = other[-1][...]

    @on(me_ref[0], roles)
    def _():
        half = half_of(me_ref[0])
        cols = [half_columns(half, h, heads) for h in range(heads)]

        def mixed_of(h):
            earlier = total(e_refs, head(h))
            earlier_ref[head(h), :] = earlier
            return intra_ref[:, cols[h]] + dot_nn(q_ref[:, cols[h]], earlier)

        def put_state(h, grad):
            state = dot_nn(qt_ref[cols[h], :], grad).astype(BF16)
            for ref in state_refs:
                ref[head(h), :] = state

        mixed, last = mixed_of(0), None
        for h in range(heads):
            ahead = mixed_of(h + 1) if h + 1 < heads else None
            g = g_ref[:, cols[h]].astype(F32)
            squares = jnp.mean(mixed * mixed, axis=-1, keepdims=True)
            along = jnp.mean(g * mixed, axis=-1, keepdims=True)
            if h:
                put_state(h - 1, last)
            inverse = lax.rsqrt(squares + norm_eps)
            normed = mixed * inverse
            last = (inverse * (g - normed * (along * inverse))).astype(BF16)
            grad_ref[:, head(h)] = last
            normed_ref[:, head(h)] = normed.astype(BF16)
            mixed = ahead
        put_state(heads - 1, last)


def mid(half_of, roles, me, shared, token, earlier, keep=(), other=()):
    merge = len(other) - len(keep)
    length, width = shared[0].shape
    half_shape = jax.ShapeDtypeStruct((length, width // 2), BF16)
    state_shape = jax.ShapeDtypeStruct(earlier[0].shape, BF16)
    normed, grad, low, token, *states_out = pl.pallas_call(
        functools.partial(mid_kernel, half_of, roles, keep, merge),
        in_specs=[SMEM_SPEC] + [VMEM_SPEC] * (5 + len(other) + len(earlier)),
        out_specs=(VMEM_SPEC,) * (5 + merge),
        **params("mid", (half_shape, half_shape, state_shape, TOKEN) + (state_shape,) * (1 + merge)),
    )(me, *shared, token, *other, *earlier)
    return (normed, grad, low), *states_out, token


def back_kernel(half_of, roles, sets, me_ref, q_ref, k_ref, v_ref, token_ref, *refs):
    normed_ref, gq_ref, gk_ref, gv_ref, done_ref, gq_buf, n_buf, gq_sem, n_sem = refs[-9:]
    length = q_ref.shape[0]
    rows = lax.broadcasted_iota(jnp.int32, (length, length), 0)
    columns = lax.broadcasted_iota(jnp.int32, (length, length), 1)
    mask, mask_t = columns <= rows, rows <= columns
    heads = gk_ref.shape[1] // DH
    half = half_of(me_ref[0])

    def chosen(index, place):
        value = refs[index][place]
        if sets > 1:
            value = jnp.where(among(me_ref[0], roles), refs[3 + index][place], value)
        return value

    n_buf[...] = chosen(0, (slice(None), slice(None)))
    normed_copy = half_copy(half, n_buf, normed_ref, n_sem)
    normed_copy.start()
    for h in range(heads):
        cols = half_columns(half, h, heads)
        q, k, v = (ref[:, cols] for ref in (q_ref, k_ref, v_ref))
        grad = chosen(1, (slice(None), head(h)))
        earlier = chosen(2, (head(h), slice(None)))
        scores_t = jnp.where(mask_t, dot_nt(k, q), 0.0).astype(BF16)
        grad_scores = jnp.where(mask, dot_nt(grad, v), 0.0).astype(BF16)
        grad_scores_t = jnp.where(mask_t, dot_nt(v, grad), 0.0).astype(BF16)
        gq_buf[:, head(h)] = (dot_nn(grad_scores, k) + dot_nt(grad, earlier)).astype(BF16)
        gk_ref[:, head(h)] = dot_nn(grad_scores_t, q)
        gv_ref[:, head(h)] = dot_nn(scores_t, grad)
    done_ref[...] = token_ref[...]
    gq_copy = half_copy(half, gq_buf, gq_ref, gq_sem)
    gq_copy.start()
    normed_copy.wait()
    gq_copy.wait()


def back(half_of, roles, me, q, k, v, token, sets, filled=()):
    length, width = q.shape
    whole = jax.ShapeDtypeStruct(q.shape, BF16)
    half_shape = jax.ShapeDtypeStruct((length, width // 2), F32)
    first = 5 + 3 * len(sets)
    buffers = pltpu.VMEM((length, width // 2), BF16)
    return pl.pallas_call(
        functools.partial(back_kernel, half_of, roles, len(sets)),
        in_specs=[SMEM_SPEC] + [VMEM_SPEC] * (first - 1) + [HBM_SPEC] * len(filled),
        out_specs=(HBM_SPEC, HBM_SPEC, VMEM_SPEC, VMEM_SPEC, VMEM_SPEC),
        scratch_shapes=[buffers, buffers] + [pltpu.SemaphoreType.DMA] * 2,
        input_output_aliases={first: 0, first + 1: 1} if filled else {},
        **params("back", (whole, whole, half_shape, half_shape, TOKEN)),
    )(me, q, k, v, token, *(x for one in sets for x in one), *filled)


def post_first_kernel(half_of, parts, *refs):
    refs[-5][...] = refs[5][...]
    post_kernel(half_of, parts, *refs[:-5], *refs[-4:])


def post_kernel(half_of, parts, me_ref, k_ref, v_ref, gk_in_ref, gv_in_ref, token_ref, *refs):
    l_refs, (gk_ref, gv_ref, gk_buf, gv_buf, gk_sem, gv_sem) = refs[:parts], refs[-6:]
    heads = gk_in_ref.shape[1] // DH
    half = half_of(me_ref[0])
    laters = [total(l_refs, head(h)) for h in range(heads)]
    for h in range(heads):
        v = v_ref[:, half_columns(half, h, heads)]
        gk_buf[:, head(h)] = (gk_in_ref[:, head(h)] + dot_nt(v, laters[h])).astype(BF16)
    gk_copy = half_copy(half, gk_buf, gk_ref, gk_sem)
    gk_copy.start()
    for h in range(heads):
        k = k_ref[:, half_columns(half, h, heads)]
        gv_buf[:, head(h)] = (gv_in_ref[:, head(h)] + dot_nn(k, laters[h])).astype(BF16)
    gv_copy = half_copy(half, gv_buf, gv_ref, gv_sem)
    gv_copy.start()
    gk_copy.wait()
    gv_copy.wait()


def post(half_of, me, k, v, gk_in, gv_in, token, later, filled=()):
    length, width = k.shape
    first = 6 + len(later)
    whole = jax.ShapeDtypeStruct(k.shape, BF16)
    return pl.pallas_call(
        functools.partial(post_kernel if filled else post_first_kernel, half_of, len(later)),
        in_specs=[SMEM_SPEC] + [VMEM_SPEC] * (first - 1) + [HBM_SPEC] * len(filled),
        out_specs=(HBM_SPEC, HBM_SPEC) if filled else (HBM_SPEC, HBM_SPEC, VMEM_SPEC),
        scratch_shapes=[pltpu.VMEM((length, width // 2), BF16)] * 2 + [pltpu.SemaphoreType.DMA] * 2,
        input_output_aliases={first: 0, first + 1: 1} if filled else {},
        **params("post", (whole, whole) if filled else (whole, whole, TOKEN)),
    )(me, k, v, gk_in, gv_in, token, *later, *filled)


def even_half(me):
    return 1 - lax.rem(me, 2)


def odd_half(me):
    return lax.rem(me, 2)


def rows_of(array):
    return array.reshape(array.shape[1:])


def shards_four(queries, key_vectors, value_vectors, grad_output):
    out_shape = queries.shape
    q, k, v, g = (rows_of(x) for x in (queries, key_vectors, value_vectors, grad_output))
    me = lax.axis_index("ctx").astype(jnp.int32).reshape(1)
    token = jnp.zeros(TOKEN.shape, TOKEN.dtype)

    def send(x, pairs):
        return lax.ppermute(x, "ctx", pairs)

    s_a, token = states((((0,), ((0, 0),)),), me, k, v, token)
    r_a = send(s_a, [(0, 1)])
    s_b, token = near_states(1, (0, 1), me, k, v, token)
    r_b = send(s_b, [(1, 2)])
    s_c, token = near_states(0, (1, 2), me, k, v, token, (0,), (s_b,))
    r_c = send(s_c, [(0, 2), (2, 3)])
    intra_out, qt, token = intra(q, k, v, token)
    shared = (q, qt, g, intra_out)
    s12, token = add(token, r_a, s_c)
    r_far = send(s12, [(1, 3)])
    s_y, token, s12 = near_states(1, (2,), me, k, v, token, passed=(s12,))
    r_near = send(s12, [(0, 1), (1, 2)])
    r_b, token = add(token, r_b)
    s123, token = add(token, r_b, r_c, s_y)
    first, g_first, token = mid(even_half, (0, 1, 2), me, shared, token, (r_a, r_b, r_c))
    r_last = send(s123, [(2, 3)])
    first_end, g_one, token = mid(even_half, (3,), me, shared, token, (r_c, r_far), (2,), (g_first,))
    u_one = send(g_one, [(3, 2), (2, 1)])
    second, g_rest, token = mid(odd_half, (0, 1, 2), me, shared, token, (r_near,))
    second_end, g_two, g_second, token = mid(odd_half, (3,), me, shared, token, (r_last,), (1,), (g_first, g_rest))
    u_two = send(g_two, [(3, 1), (1, 0)])
    normed, grad_q, gk_second, gv_second, token = back(odd_half, (3,), me, q, k, v, token, (second, second_end))
    g12, token = add(token, u_one, g_second)
    w_far = send(g12, [(2, 0)])
    w_near = send(g12, [(3, 2), (2, 1)])
    g123, token = add(token, u_one, u_two, g_second)
    w_last = send(g123, [(1, 0)])
    normed, grad_q, gk_first, gv_first, token = back(
        even_half, (3,), me, q, k, v, token, (first, first_end), (normed, grad_q)
    )
    *filled, token = post(odd_half, me, k, v, gk_second, gv_second, token, (u_one, u_two, w_far))
    l_near, token = add(token, w_near)
    grad_k, grad_v = post(even_half, me, k, v, gk_first, gv_first, token, (l_near, w_last), filled)
    return tuple(x.reshape(out_shape) for x in (normed, grad_q, grad_k, grad_v))


def scan_states(first, second, count, backward):
    rows = first.shape[0] * 2
    shares = jnp.concatenate([first, second], axis=0).reshape(count, rows // count, DH)
    shares = lax.all_to_all(shares, "ctx", split_axis=0, concat_axis=0, tiled=True).astype(F32)
    running = jnp.cumsum(shares, axis=0)
    sums = running[-1:] - running if backward else running - shares
    sums = lax.all_to_all(sums.astype(BF16), "ctx", split_axis=0, concat_axis=0, tiled=True)
    sums = sums.reshape(rows, DH)
    return sums[: rows // 2], sums[rows // 2 :]


def low_half(me):
    return 0


def high_half(me):
    return 1


def shards_any(count, queries, key_vectors, value_vectors, grad_output):
    out_shape = queries.shape
    q, k, v, g = (rows_of(x) for x in (queries, key_vectors, value_vectors, grad_output))
    me = lax.axis_index("ctx").astype(jnp.int32).reshape(1)
    token = jnp.zeros(TOKEN.shape, TOKEN.dtype)
    s1, s2, token = states((((), ((0, 0), (1, 1))),), me, k, v, token)
    e1, e2 = scan_states(s1, s2, count, False)
    intra_out, qt, token = intra(q, k, v, token)
    shared = (q, qt, g, intra_out)
    low, g1, token = mid(low_half, (), me, shared, token, (e1,))
    high, g2, token = mid(high_half, (), me, shared, token, (e2,))
    l1, l2 = scan_states(g1, g2, count, True)
    normed, grad_q, gk1, gv1, token = back(low_half, (), me, q, k, v, token, (low,))
    normed, grad_q, gk2, gv2, token = back(high_half, (), me, q, k, v, token, (high,), (normed, grad_q))
    *filled, token = post(low_half, me, k, v, gk1, gv1, token, (l1,))
    grad_k, grad_v = post(high_half, me, k, v, gk2, gv2, token, (l2,), filled)
    return tuple(x.reshape(out_shape) for x in (normed, grad_q, grad_k, grad_v))


def solution(mesh):
    placed = P(("groups", "dp"), "ctx", "tp")
    count = mesh.shape["ctx"]

    def shards(*args):
        if count == 4:
            return shards_four(*args)
        return shards_any(count, *args)

    return jax.shard_map(
        shards,
        mesh=mesh,
        in_specs=(placed,) * 4,
        out_specs=(placed,) * 4,
        check_vma=False,
    )
```

```python
import functools

import jax
import jax.numpy as jnp
from jax import lax
from jax.experimental import pallas as pl
from jax.experimental.pallas import tpu as pltpu
from jax.sharding import PartitionSpec as P

DH = 128
norm_eps = 1e-06
F32 = jnp.float32
BF16 = jnp.bfloat16

VMEM_SPEC = pl.BlockSpec(memory_space=pltpu.VMEM)
HBM_SPEC = pl.BlockSpec(memory_space=pltpu.HBM)
SMEM_SPEC = pl.BlockSpec(memory_space=pltpu.SMEM)
COST = pl.CostEstimate(flops=0, transcendentals=0, bytes_accessed=4096)
PARAMS = pltpu.CompilerParams(vmem_limit_bytes=16 << 20)


def params(name, parts):
    return dict(compiler_params=PARAMS, cost_estimate=COST, name=name, out_shape=parts)


def dot_nn(a, b):
    return lax.dot_general(a, b, (((1,), (0,)), ((), ())), preferred_element_type=F32)


def dot_nt(a, b):
    return lax.dot_general(a, b, (((1,), (1,)), ((), ())), preferred_element_type=F32)


def dot_tn(a, b):
    return lax.dot_general(a, b, (((0,), (0,)), ((), ())), preferred_element_type=F32)


def head(index):
    return slice(index * DH, (index + 1) * DH)


def causal(length):
    rows = lax.broadcasted_iota(jnp.int32, (length, length), 0)
    columns = lax.broadcasted_iota(jnp.int32, (length, length), 1)
    return columns <= rows


def half_columns(half, h, heads):
    return pl.ds(pl.multiple_of((half * heads + h) * DH, DH), DH)


def among(me, roles):
    hit = me == roles[0]
    for role in roles[1:]:
        hit = hit | (me == role)
    return hit


def on(me, roles):
    return pl.when(among(me, roles)) if roles else lambda body: body()


def near_state_kernel(half, roles, keep, me_ref, k_ref, v_ref, token_ref, *refs):
    passed = (len(refs) - 2 - len(keep)) // 2
    out_ref, done_ref, *copies = refs[-2 - passed :]
    heads = out_ref.shape[0] // DH
    done_ref[...] = token_ref[...]
    for source, copy in zip(refs[len(keep) :], copies):
        copy[...] = source[...]
    if keep:

        @on(me_ref[0], keep)
        def _():
            out_ref[...] = refs[0][...]

    @on(me_ref[0], roles)
    def _():
        for h in range(heads):
            cols = head(half * heads + h)
            out_ref[head(h), :] = dot_tn(k_ref[:, cols], v_ref[:, cols]).astype(BF16)


def near_states(half, roles, me, k, v, token, keep=(), spare=(), passed=()):
    shape = jax.ShapeDtypeStruct((k.shape[1] // 2, DH), BF16)
    return pl.pallas_call(
        functools.partial(near_state_kernel, half, roles, keep),
        in_specs=[SMEM_SPEC] + [VMEM_SPEC] * (3 + len(spare) + len(passed)),
        out_specs=(VMEM_SPEC,) * (2 + len(passed)),
        **params("near_states", (shape, TOKEN) + (shape,) * len(passed)),
    )(me, k, v, token, *spare, *passed)


def state_kernel(half, roles, me_ref, k_ref, v_ref, token_ref, out_ref, done_ref, k_buf, v_buf, k_sem, v_sem):
    width = k_buf.shape[1]
    heads = width // DH
    done_ref[...] = token_ref[...]

    @on(me_ref[0], roles)
    def _():
        cols = slice(half * width, (half + 1) * width)
        copies = (
            pltpu.make_async_copy(k_ref.at[:, cols], k_buf, k_sem),
            pltpu.make_async_copy(v_ref.at[:, cols], v_buf, v_sem),
        )
        for copy in copies:
            copy.start()
        for copy in copies:
            copy.wait()
        for h in range(heads):
            out_ref[head(h), :] = dot_tn(k_buf[:, head(h)], v_buf[:, head(h)]).astype(BF16)


def states(half, roles, me, k, v, token):
    length, width = k.shape
    k, v = (pltpu.with_memory_space_constraint(x, pltpu.HBM) for x in (k, v))
    return pl.pallas_call(
        functools.partial(state_kernel, half, roles),
        in_specs=[SMEM_SPEC, HBM_SPEC, HBM_SPEC, VMEM_SPEC],
        out_specs=(VMEM_SPEC,) * 2,
        scratch_shapes=[pltpu.VMEM((length, width // 2), BF16)] * 2 + [pltpu.SemaphoreType.DMA] * 2,
        **params("states", (jax.ShapeDtypeStruct((width // 2, DH), BF16), TOKEN)),
    )(me, k, v, token)


TOKEN = jax.ShapeDtypeStruct((8, DH), F32)


def intra_kernel(q_ref, k_ref, v_ref, token_ref, out_ref, qt_ref, done_ref):
    mask = causal(q_ref.shape[0])
    heads = q_ref.shape[1] // DH

    def scores_of(h):
        return jnp.where(mask, dot_nt(q_ref[:, head(h)], k_ref[:, head(h)]), 0.0).astype(BF16)

    scores = scores_of(0)
    for h in range(heads):
        ahead = scores_of(h + 1) if h + 1 < heads else None
        out_ref[:, head(h)] = dot_nn(scores, v_ref[:, head(h)])
        qt_ref[head(h), :] = q_ref[:, head(h)].T
        scores = ahead
    done_ref[...] = token_ref[...]


def intra(q, k, v, token):
    length, width = q.shape
    return pl.pallas_call(
        intra_kernel,
        in_specs=[VMEM_SPEC] * 4,
        out_specs=(VMEM_SPEC,) * 3,
        **params("intra", (jax.ShapeDtypeStruct(q.shape, F32), jax.ShapeDtypeStruct((width, length), BF16), TOKEN)),
    )(q, k, v, token)


def total(refs, rows=slice(None)):
    value = refs[0][rows, :].astype(F32)
    for ref in refs[1:]:
        value = value + ref[rows, :].astype(F32)
    return value.astype(BF16)


def add_kernel(token_ref, *refs):
    refs[-2][...] = total(refs[:-2])
    refs[-1][...] = token_ref[...]


def add(token, *arrays):
    return pl.pallas_call(
        add_kernel,
        in_specs=[VMEM_SPEC] * (1 + len(arrays)),
        out_specs=(VMEM_SPEC,) * 2,
        **params("add", (jax.ShapeDtypeStruct(arrays[0].shape, BF16), TOKEN)),
    )(token, *arrays)


def half_columns(half, h, heads):
    return pl.ds(pl.multiple_of((half * heads + h) * DH, DH), DH)


def half_copy(half, buf, ref, sem):
    width = buf.shape[1]
    return pltpu.make_async_copy(buf, ref.at[:, pl.ds(pl.multiple_of(half * width, width), width)], sem)


def mid_kernel(half_of, roles, keep, merge, me_ref, q_ref, qt_ref, g_ref, intra_ref, token_ref, *refs):
    normed_ref, grad_ref, earlier_ref, done_ref, *state_refs = refs[-5 - merge :]
    other, e_refs = refs[: len(keep) + merge], refs[len(keep) + merge : -5 - merge]
    state_ref = state_refs[0]
    heads = state_ref.shape[0] // DH
    done_ref[...] = token_ref[...]
    if keep:

        @on(me_ref[0], keep)
        def _():
            state_ref[...] = other[0][...]

    if merge:

        @pl.when(jnp.logical_not(among(me_ref[0], roles)))
        def _():
            state_refs[1][...] = other[-1][...]

    @on(me_ref[0], roles)
    def _():
        half = half_of(me_ref[0])
        cols = [half_columns(half, h, heads) for h in range(heads)]

        def mixed_of(h):
            earlier = total(e_refs, head(h))
            earlier_ref[head(h), :] = earlier
            return intra_ref[:, cols[h]] + dot_nn(q_ref[:, cols[h]], earlier)

        def put_state(h, grad):
            state = dot_nn(qt_ref[cols[h], :], grad).astype(BF16)
            for ref in state_refs:
                ref[head(h), :] = state

        mixed, last = mixed_of(0), None
        for h in range(heads):
            ahead = mixed_of(h + 1) if h + 1 < heads else None
            g = g_ref[:, cols[h]].astype(F32)
            squares = jnp.mean(mixed * mixed, axis=-1, keepdims=True)
            along = jnp.mean(g * mixed, axis=-1, keepdims=True)
            if h:
                put_state(h - 1, last)
            inverse = lax.rsqrt(squares + norm_eps)
            normed = mixed * inverse
            last = (inverse * (g - normed * (along * inverse))).astype(BF16)
            grad_ref[:, head(h)] = last
            normed_ref[:, head(h)] = normed.astype(BF16)
            mixed = ahead
        put_state(heads - 1, last)


def mid(half_of, roles, me, shared, token, earlier, keep=(), other=()):
    merge = len(other) - len(keep)
    length, width = shared[0].shape
    half_shape = jax.ShapeDtypeStruct((length, width // 2), BF16)
    state_shape = jax.ShapeDtypeStruct(earlier[0].shape, BF16)
    normed, grad, low, token, *states_out = pl.pallas_call(
        functools.partial(mid_kernel, half_of, roles, keep, merge),
        in_specs=[SMEM_SPEC] + [VMEM_SPEC] * (5 + len(other) + len(earlier)),
        out_specs=(VMEM_SPEC,) * (5 + merge),
        **params("mid", (half_shape, half_shape, state_shape, TOKEN) + (state_shape,) * (1 + merge)),
    )(me, *shared, token, *other, *earlier)
    return (normed, grad, low), *states_out, token


def back_kernel(half_of, roles, sets, me_ref, q_ref, k_ref, v_ref, token_ref, *refs):
    normed_ref, gq_ref, gk_ref, gv_ref, done_ref, gq_buf, n_buf, gq_sem, n_sem = refs[-9:]
    length = q_ref.shape[0]
    rows = lax.broadcasted_iota(jnp.int32, (length, length), 0)
    columns = lax.broadcasted_iota(jnp.int32, (length, length), 1)
    mask, mask_t = columns <= rows, rows <= columns
    heads = gk_ref.shape[1] // DH
    half = half_of(me_ref[0])

    def chosen(index, place):
        value = refs[index][place]
        if sets > 1:
            value = jnp.where(among(me_ref[0], roles), refs[3 + index][place], value)
        return value

    n_buf[...] = chosen(0, (slice(None), slice(None)))
    normed_copy = half_copy(half, n_buf, normed_ref, n_sem)
    normed_copy.start()
    for h in range(heads):
        cols = half_columns(half, h, heads)
        q, k, v = (ref[:, cols] for ref in (q_ref, k_ref, v_ref))
        grad = chosen(1, (slice(None), head(h)))
        earlier = chosen(2, (head(h), slice(None)))
        scores_t = jnp.where(mask_t, dot_nt(k, q), 0.0).astype(BF16)
        grad_scores = jnp.where(mask, dot_nt(grad, v), 0.0).astype(BF16)
        grad_scores_t = jnp.where(mask_t, dot_nt(v, grad), 0.0).astype(BF16)
        gq_buf[:, head(h)] = (dot_nn(grad_scores, k) + dot_nt(grad, earlier)).astype(BF16)
        gk_ref[:, head(h)] = dot_nn(grad_scores_t, q)
        gv_ref[:, head(h)] = dot_nn(scores_t, grad)
    done_ref[...] = token_ref[...]
    gq_copy = half_copy(half, gq_buf, gq_ref, gq_sem)
    gq_copy.start()
    normed_copy.wait()
    gq_copy.wait()


def back(half_of, roles, me, q, k, v, token, sets, filled=()):
    length, width = q.shape
    whole = jax.ShapeDtypeStruct(q.shape, BF16)
    half_shape = jax.ShapeDtypeStruct((length, width // 2), F32)
    first = 5 + 3 * len(sets)
    buffers = pltpu.VMEM((length, width // 2), BF16)
    return pl.pallas_call(
        functools.partial(back_kernel, half_of, roles, len(sets)),
        in_specs=[SMEM_SPEC] + [VMEM_SPEC] * (first - 1) + [HBM_SPEC] * len(filled),
        out_specs=(HBM_SPEC, HBM_SPEC, VMEM_SPEC, VMEM_SPEC, VMEM_SPEC),
        scratch_shapes=[buffers, buffers] + [pltpu.SemaphoreType.DMA] * 2,
        input_output_aliases={first: 0, first + 1: 1} if filled else {},
        **params("back", (whole, whole, half_shape, half_shape, TOKEN)),
    )(me, q, k, v, token, *(x for one in sets for x in one), *filled)


def post_first_kernel(half_of, parts, *refs):
    refs[-5][...] = refs[5][...]
    post_kernel(half_of, parts, *refs[:-5], *refs[-4:])


def post_kernel(half_of, parts, me_ref, k_ref, v_ref, gk_in_ref, gv_in_ref, token_ref, *refs):
    l_refs, (gk_ref, gv_ref, gk_buf, gv_buf, gk_sem, gv_sem) = refs[:parts], refs[-6:]
    heads = gk_in_ref.shape[1] // DH
    half = half_of(me_ref[0])
    laters = [total(l_refs, head(h)) for h in range(heads)]
    for h in range(heads):
        v = v_ref[:, half_columns(half, h, heads)]
        gk_buf[:, head(h)] = (gk_in_ref[:, head(h)] + dot_nt(v, laters[h])).astype(BF16)
    gk_copy = half_copy(half, gk_buf, gk_ref, gk_sem)
    gk_copy.start()
    for h in range(heads):
        k = k_ref[:, half_columns(half, h, heads)]
        gv_buf[:, head(h)] = (gv_in_ref[:, head(h)] + dot_nn(k, laters[h])).astype(BF16)
    gv_copy = half_copy(half, gv_buf, gv_ref, gv_sem)
    gv_copy.start()
    gk_copy.wait()
    gv_copy.wait()


def post(half_of, me, k, v, gk_in, gv_in, token, later, filled=()):
    length, width = k.shape
    first = 6 + len(later)
    whole = jax.ShapeDtypeStruct(k.shape, BF16)
    return pl.pallas_call(
        functools.partial(post_kernel if filled else post_first_kernel, half_of, len(later)),
        in_specs=[SMEM_SPEC] + [VMEM_SPEC] * (first - 1) + [HBM_SPEC] * len(filled),
        out_specs=(HBM_SPEC, HBM_SPEC) if filled else (HBM_SPEC, HBM_SPEC, VMEM_SPEC),
        scratch_shapes=[pltpu.VMEM((length, width // 2), BF16)] * 2 + [pltpu.SemaphoreType.DMA] * 2,
        input_output_aliases={first: 0, first + 1: 1} if filled else {},
        **params("post", (whole, whole) if filled else (whole, whole, TOKEN)),
    )(me, k, v, gk_in, gv_in, token, *later, *filled)


def even_half(me):
    return 1 - lax.rem(me, 2)


def odd_half(me):
    return lax.rem(me, 2)


def rows_of(array):
    return array.reshape(array.shape[1:])


def shards_four(queries, key_vectors, value_vectors, grad_output):
    out_shape = queries.shape
    q, k, v, g = (rows_of(x) for x in (queries, key_vectors, value_vectors, grad_output))
    me = lax.axis_index("ctx").astype(jnp.int32).reshape(1)
    token = jnp.zeros(TOKEN.shape, TOKEN.dtype)

    def send(x, pairs):
        return lax.ppermute(x, "ctx", pairs)

    s_a, token = states(0, (0,), me, k, v, token)
    r_a = send(s_a, [(0, 1)])
    s_b, token = states(1, (0, 1), me, k, v, token)
    r_b = send(s_b, [(1, 2)])
    s_c, token = near_states(0, (1, 2), me, k, v, token, (0,), (s_b,))
    r_c = send(s_c, [(0, 2), (2, 3)])
    intra_out, qt, token = intra(q, k, v, token)
    shared = (q, qt, g, intra_out)
    s12, token = add(token, r_a, s_c)
    r_far = send(s12, [(1, 3)])
    s_y, token, s12 = near_states(1, (2,), me, k, v, token, passed=(s12,))
    r_near = send(s12, [(0, 1), (1, 2)])
    r_b, token = add(token, r_b)
    s123, token = add(token, r_b, r_c, s_y)
    first, g_first, token = mid(even_half, (0, 1, 2), me, shared, token, (r_a, r_b, r_c))
    r_last = send(s123, [(2, 3)])
    first_end, g_one, token = mid(even_half, (3,), me, shared, token, (r_c, r_far), (2,), (g_first,))
    u_one = send(g_one, [(3, 2), (2, 1)])
    second, g_rest, token = mid(odd_half, (0, 1, 2), me, shared, token, (r_near,))
    second_end, g_two, g_second, token = mid(odd_half, (3,), me, shared, token, (r_last,), (1,), (g_first, g_rest))
    u_two = send(g_two, [(3, 1), (1, 0)])
    normed, grad_q, gk_second, gv_second, token = back(odd_half, (3,), me, q, k, v, token, (second, second_end))
    g12, token = add(token, u_one, g_second)
    w_far = send(g12, [(2, 0)])
    w_near = send(g12, [(3, 2), (2, 1)])
    g123, token = add(token, u_one, u_two, g_second)
    w_last = send(g123, [(1, 0)])
    normed, grad_q, gk_first, gv_first, token = back(
        even_half, (3,), me, q, k, v, token, (first, first_end), (normed, grad_q)
    )
    *filled, token = post(odd_half, me, k, v, gk_second, gv_second, token, (u_one, u_two, w_far))
    l_near, token = add(token, w_near)
    grad_k, grad_v = post(even_half, me, k, v, gk_first, gv_first, token, (l_near, w_last), filled)
    return tuple(x.reshape(out_shape) for x in (normed, grad_q, grad_k, grad_v))


def scan_states(first, second, count, backward):
    rows = first.shape[0] * 2
    shares = jnp.concatenate([first, second], axis=0).reshape(count, rows // count, DH)
    shares = lax.all_to_all(shares, "ctx", split_axis=0, concat_axis=0, tiled=True).astype(F32)
    running = jnp.cumsum(shares, axis=0)
    sums = running[-1:] - running if backward else running - shares
    sums = lax.all_to_all(sums.astype(BF16), "ctx", split_axis=0, concat_axis=0, tiled=True)
    sums = sums.reshape(rows, DH)
    return sums[: rows // 2], sums[rows // 2 :]


def low_half(me):
    return 0


def high_half(me):
    return 1


def shards_any(count, queries, key_vectors, value_vectors, grad_output):
    out_shape = queries.shape
    q, k, v, g = (rows_of(x) for x in (queries, key_vectors, value_vectors, grad_output))
    me = lax.axis_index("ctx").astype(jnp.int32).reshape(1)
    token = jnp.zeros(TOKEN.shape, TOKEN.dtype)
    s1, token = near_states(0, (), me, k, v, token)
    s2, token = near_states(1, (), me, k, v, token)
    e1, e2 = scan_states(s1, s2, count, False)
    intra_out, qt, token = intra(q, k, v, token)
    shared = (q, qt, g, intra_out)
    low, g1, token = mid(low_half, (), me, shared, token, (e1,))
    high, g2, token = mid(high_half, (), me, shared, token, (e2,))
    l1, l2 = scan_states(g1, g2, count, True)
    normed, grad_q, gk1, gv1, token = back(low_half, (), me, q, k, v, token, (low,))
    normed, grad_q, gk2, gv2, token = back(high_half, (), me, q, k, v, token, (high,), (normed, grad_q))
    *filled, token = post(low_half, me, k, v, gk1, gv1, token, (l1,))
    grad_k, grad_v = post(high_half, me, k, v, gk2, gv2, token, (l2,), filled)
    return tuple(x.reshape(out_shape) for x in (normed, grad_q, grad_k, grad_v))


def solution(mesh):
    placed = P(("groups", "dp"), "ctx", "tp")
    count = mesh.shape["ctx"]

    def shards(*args):
        if count == 4:
            return shards_four(*args)
        return shards_any(count, *args)

    return jax.shard_map(
        shards,
        mesh=mesh,
        in_specs=(placed,) * 4,
        out_specs=(placed,) * 4,
        check_vma=False,
    )
```

```python
import functools

import jax
import jax.numpy as jnp
from jax import lax
from jax.experimental import pallas as pl
from jax.experimental.pallas import tpu as pltpu
from jax.sharding import PartitionSpec as P

DH = 128
norm_eps = 1e-06
F32 = jnp.float32
BF16 = jnp.bfloat16

VMEM_SPEC = pl.BlockSpec(memory_space=pltpu.VMEM)
HBM_SPEC = pl.BlockSpec(memory_space=pltpu.HBM)
SMEM_SPEC = pl.BlockSpec(memory_space=pltpu.SMEM)
COST = pl.CostEstimate(flops=0, transcendentals=0, bytes_accessed=4096)
PARAMS = pltpu.CompilerParams(vmem_limit_bytes=16 << 20)


def params(name, parts):
    return dict(compiler_params=PARAMS, cost_estimate=COST, name=name, out_shape=parts)


def dot_nn(a, b):
    return lax.dot_general(a, b, (((1,), (0,)), ((), ())), preferred_element_type=F32)


def dot_nt(a, b):
    return lax.dot_general(a, b, (((1,), (1,)), ((), ())), preferred_element_type=F32)


def dot_tn(a, b):
    return lax.dot_general(a, b, (((0,), (0,)), ((), ())), preferred_element_type=F32)


def head(index):
    return slice(index * DH, (index + 1) * DH)


def causal(length):
    rows = lax.broadcasted_iota(jnp.int32, (length, length), 0)
    columns = lax.broadcasted_iota(jnp.int32, (length, length), 1)
    return columns <= rows


def half_columns(half, h, heads):
    return pl.ds(pl.multiple_of((half * heads + h) * DH, DH), DH)


def among(me, roles):
    hit = me == roles[0]
    for role in roles[1:]:
        hit = hit | (me == role)
    return hit


def on(me, roles):
    return pl.when(among(me, roles)) if roles else lambda body: body()


def near_state_kernel(half, roles, keep, me_ref, k_ref, v_ref, token_ref, *refs):
    passed = (len(refs) - 2 - len(keep)) // 2
    out_ref, done_ref, *copies = refs[-2 - passed :]
    heads = out_ref.shape[0] // DH
    done_ref[...] = token_ref[...]
    for source, copy in zip(refs[len(keep) :], copies):
        copy[...] = source[...]
    if keep:

        @on(me_ref[0], keep)
        def _():
            out_ref[...] = refs[0][...]

    @on(me_ref[0], roles)
    def _():
        for h in range(heads):
            cols = head(half * heads + h)
            out_ref[head(h), :] = dot_tn(k_ref[:, cols], v_ref[:, cols]).astype(BF16)


def near_states(half, roles, me, k, v, token, keep=(), spare=(), passed=()):
    shape = jax.ShapeDtypeStruct((k.shape[1] // 2, DH), BF16)
    return pl.pallas_call(
        functools.partial(near_state_kernel, half, roles, keep),
        in_specs=[SMEM_SPEC] + [VMEM_SPEC] * (3 + len(spare) + len(passed)),
        out_specs=(VMEM_SPEC,) * (2 + len(passed)),
        **params("near_states", (shape, TOKEN) + (shape,) * len(passed)),
    )(me, k, v, token, *spare, *passed)


def state_kernel(halves, roles, keep, me_ref, k_ref, v_ref, token_ref, *refs):
    done_ref, k_buf, v_buf, k_sem, v_sem = refs[-5:]
    outs = refs[len(keep) : -5]
    width = k_buf.shape[2]
    heads = width // DH
    done_ref[...] = token_ref[...]
    if keep:

        @on(me_ref[0], keep)
        def _():
            outs[0][...] = refs[0][...]

    @on(me_ref[0], roles)
    def _():
        copies = []
        for slot, half in enumerate(halves):
            cols = slice(half * width, (half + 1) * width)
            copies.append(pltpu.make_async_copy(k_ref.at[:, cols], k_buf.at[slot], k_sem.at[slot]))
            copies.append(pltpu.make_async_copy(v_ref.at[:, cols], v_buf.at[slot], v_sem.at[slot]))
        for copy in copies:
            copy.start()
        for copy in copies:
            copy.wait()
        for slot, out_ref in enumerate(outs):
            for h in range(heads):
                out_ref[head(h), :] = dot_tn(k_buf[slot, :, head(h)], v_buf[slot, :, head(h)]).astype(BF16)


def states(halves, roles, me, k, v, token, keep=(), spare=()):
    length, width = k.shape
    count = len(halves)
    k, v = (pltpu.with_memory_space_constraint(x, pltpu.HBM) for x in (k, v))
    shape = jax.ShapeDtypeStruct((width // 2, DH), BF16)
    return pl.pallas_call(
        functools.partial(state_kernel, halves, roles, keep),
        in_specs=[SMEM_SPEC, HBM_SPEC, HBM_SPEC] + [VMEM_SPEC] * (1 + len(spare)),
        out_specs=(VMEM_SPEC,) * (count + 1),
        scratch_shapes=[pltpu.VMEM((count, length, width // 2), BF16)] * 2 + [pltpu.SemaphoreType.DMA((count,))] * 2,
        **params("states", (shape,) * count + (TOKEN,)),
    )(me, k, v, token, *spare)


TOKEN = jax.ShapeDtypeStruct((8, DH), F32)


def intra_kernel(q_ref, k_ref, v_ref, token_ref, out_ref, qt_ref, done_ref):
    mask = causal(q_ref.shape[0])
    heads = q_ref.shape[1] // DH

    def scores_of(h):
        return jnp.where(mask, dot_nt(q_ref[:, head(h)], k_ref[:, head(h)]), 0.0).astype(BF16)

    scores = scores_of(0)
    for h in range(heads):
        ahead = scores_of(h + 1) if h + 1 < heads else None
        out_ref[:, head(h)] = dot_nn(scores, v_ref[:, head(h)])
        qt_ref[head(h), :] = q_ref[:, head(h)].T
        scores = ahead
    done_ref[...] = token_ref[...]


def intra(q, k, v, token):
    length, width = q.shape
    return pl.pallas_call(
        intra_kernel,
        in_specs=[VMEM_SPEC] * 4,
        out_specs=(VMEM_SPEC,) * 3,
        **params("intra", (jax.ShapeDtypeStruct(q.shape, F32), jax.ShapeDtypeStruct((width, length), BF16), TOKEN)),
    )(q, k, v, token)


def total(refs, rows=slice(None)):
    value = refs[0][rows, :].astype(F32)
    for ref in refs[1:]:
        value = value + ref[rows, :].astype(F32)
    return value.astype(BF16)


def add_kernel(token_ref, *refs):
    refs[-2][...] = total(refs[:-2])
    refs[-1][...] = token_ref[...]


def add(token, *arrays):
    return pl.pallas_call(
        add_kernel,
        in_specs=[VMEM_SPEC] * (1 + len(arrays)),
        out_specs=(VMEM_SPEC,) * 2,
        **params("add", (jax.ShapeDtypeStruct(arrays[0].shape, BF16), TOKEN)),
    )(token, *arrays)


def half_columns(half, h, heads):
    return pl.ds(pl.multiple_of((half * heads + h) * DH, DH), DH)


def half_copy(half, buf, ref, sem):
    width = buf.shape[1]
    return pltpu.make_async_copy(buf, ref.at[:, pl.ds(pl.multiple_of(half * width, width), width)], sem)


def mid_kernel(half_of, roles, keep, merge, me_ref, q_ref, qt_ref, g_ref, intra_ref, token_ref, *refs):
    normed_ref, grad_ref, earlier_ref, done_ref, *state_refs = refs[-5 - merge :]
    other, e_refs = refs[: len(keep) + merge], refs[len(keep) + merge : -5 - merge]
    state_ref = state_refs[0]
    heads = state_ref.shape[0] // DH
    done_ref[...] = token_ref[...]
    if keep:

        @on(me_ref[0], keep)
        def _():
            state_ref[...] = other[0][...]

    if merge:

        @pl.when(jnp.logical_not(among(me_ref[0], roles)))
        def _():
            state_refs[1][...] = other[-1][...]

    @on(me_ref[0], roles)
    def _():
        half = half_of(me_ref[0])
        cols = [half_columns(half, h, heads) for h in range(heads)]

        def mixed_of(h):
            earlier = total(e_refs, head(h))
            earlier_ref[head(h), :] = earlier
            return intra_ref[:, cols[h]] + dot_nn(q_ref[:, cols[h]], earlier)

        def put_state(h, grad):
            state = dot_nn(qt_ref[cols[h], :], grad).astype(BF16)
            for ref in state_refs:
                ref[head(h), :] = state

        mixed, last = mixed_of(0), None
        for h in range(heads):
            ahead = mixed_of(h + 1) if h + 1 < heads else None
            g = g_ref[:, cols[h]].astype(F32)
            squares = jnp.mean(mixed * mixed, axis=-1, keepdims=True)
            along = jnp.mean(g * mixed, axis=-1, keepdims=True)
            if h:
                put_state(h - 1, last)
            inverse = lax.rsqrt(squares + norm_eps)
            normed = mixed * inverse
            last = (inverse * (g - normed * (along * inverse))).astype(BF16)
            grad_ref[:, head(h)] = last
            normed_ref[:, head(h)] = normed.astype(BF16)
            mixed = ahead
        put_state(heads - 1, last)


def mid(half_of, roles, me, shared, token, earlier, keep=(), other=()):
    merge = len(other) - len(keep)
    length, width = shared[0].shape
    half_shape = jax.ShapeDtypeStruct((length, width // 2), BF16)
    state_shape = jax.ShapeDtypeStruct(earlier[0].shape, BF16)
    normed, grad, low, token, *states_out = pl.pallas_call(
        functools.partial(mid_kernel, half_of, roles, keep, merge),
        in_specs=[SMEM_SPEC] + [VMEM_SPEC] * (5 + len(other) + len(earlier)),
        out_specs=(VMEM_SPEC,) * (5 + merge),
        **params("mid", (half_shape, half_shape, state_shape, TOKEN) + (state_shape,) * (1 + merge)),
    )(me, *shared, token, *other, *earlier)
    return (normed, grad, low), *states_out, token


def back_kernel(half_of, roles, sets, me_ref, q_ref, k_ref, v_ref, token_ref, *refs):
    normed_ref, gq_ref, gk_ref, gv_ref, done_ref, gq_buf, n_buf, gq_sem, n_sem = refs[-9:]
    length = q_ref.shape[0]
    rows = lax.broadcasted_iota(jnp.int32, (length, length), 0)
    columns = lax.broadcasted_iota(jnp.int32, (length, length), 1)
    mask, mask_t = columns <= rows, rows <= columns
    heads = gk_ref.shape[1] // DH
    half = half_of(me_ref[0])

    def chosen(index, place):
        value = refs[index][place]
        if sets > 1:
            value = jnp.where(among(me_ref[0], roles), refs[3 + index][place], value)
        return value

    n_buf[...] = chosen(0, (slice(None), slice(None)))
    normed_copy = half_copy(half, n_buf, normed_ref, n_sem)
    normed_copy.start()
    for h in range(heads):
        cols = half_columns(half, h, heads)
        q, k, v = (ref[:, cols] for ref in (q_ref, k_ref, v_ref))
        grad = chosen(1, (slice(None), head(h)))
        earlier = chosen(2, (head(h), slice(None)))
        scores_t = jnp.where(mask_t, dot_nt(k, q), 0.0).astype(BF16)
        grad_scores = jnp.where(mask, dot_nt(grad, v), 0.0).astype(BF16)
        grad_scores_t = jnp.where(mask_t, dot_nt(v, grad), 0.0).astype(BF16)
        gq_buf[:, head(h)] = (dot_nn(grad_scores, k) + dot_nt(grad, earlier)).astype(BF16)
        gk_ref[:, head(h)] = dot_nn(grad_scores_t, q)
        gv_ref[:, head(h)] = dot_nn(scores_t, grad)
    done_ref[...] = token_ref[...]
    gq_copy = half_copy(half, gq_buf, gq_ref, gq_sem)
    gq_copy.start()
    normed_copy.wait()
    gq_copy.wait()


def back(half_of, roles, me, q, k, v, token, sets, filled=()):
    length, width = q.shape
    whole = jax.ShapeDtypeStruct(q.shape, BF16)
    half_shape = jax.ShapeDtypeStruct((length, width // 2), F32)
    first = 5 + 3 * len(sets)
    buffers = pltpu.VMEM((length, width // 2), BF16)
    return pl.pallas_call(
        functools.partial(back_kernel, half_of, roles, len(sets)),
        in_specs=[SMEM_SPEC] + [VMEM_SPEC] * (first - 1) + [HBM_SPEC] * len(filled),
        out_specs=(HBM_SPEC, HBM_SPEC, VMEM_SPEC, VMEM_SPEC, VMEM_SPEC),
        scratch_shapes=[buffers, buffers] + [pltpu.SemaphoreType.DMA] * 2,
        input_output_aliases={first: 0, first + 1: 1} if filled else {},
        **params("back", (whole, whole, half_shape, half_shape, TOKEN)),
    )(me, q, k, v, token, *(x for one in sets for x in one), *filled)


def post_first_kernel(half_of, parts, *refs):
    refs[-5][...] = refs[5][...]
    post_kernel(half_of, parts, *refs[:-5], *refs[-4:])


def post_kernel(half_of, parts, me_ref, k_ref, v_ref, gk_in_ref, gv_in_ref, token_ref, *refs):
    l_refs, (gk_ref, gv_ref, gk_buf, gv_buf, gk_sem, gv_sem) = refs[:parts], refs[-6:]
    heads = gk_in_ref.shape[1] // DH
    half = half_of(me_ref[0])
    laters = [total(l_refs, head(h)) for h in range(heads)]
    for h in range(heads):
        v = v_ref[:, half_columns(half, h, heads)]
        gk_buf[:, head(h)] = (gk_in_ref[:, head(h)] + dot_nt(v, laters[h])).astype(BF16)
    gk_copy = half_copy(half, gk_buf, gk_ref, gk_sem)
    gk_copy.start()
    for h in range(heads):
        k = k_ref[:, half_columns(half, h, heads)]
        gv_buf[:, head(h)] = (gv_in_ref[:, head(h)] + dot_nn(k, laters[h])).astype(BF16)
    gv_copy = half_copy(half, gv_buf, gv_ref, gv_sem)
    gv_copy.start()
    gk_copy.wait()
    gv_copy.wait()


def post(half_of, me, k, v, gk_in, gv_in, token, later, filled=()):
    length, width = k.shape
    first = 6 + len(later)
    whole = jax.ShapeDtypeStruct(k.shape, BF16)
    return pl.pallas_call(
        functools.partial(post_kernel if filled else post_first_kernel, half_of, len(later)),
        in_specs=[SMEM_SPEC] + [VMEM_SPEC] * (first - 1) + [HBM_SPEC] * len(filled),
        out_specs=(HBM_SPEC, HBM_SPEC) if filled else (HBM_SPEC, HBM_SPEC, VMEM_SPEC),
        scratch_shapes=[pltpu.VMEM((length, width // 2), BF16)] * 2 + [pltpu.SemaphoreType.DMA] * 2,
        input_output_aliases={first: 0, first + 1: 1} if filled else {},
        **params("post", (whole, whole) if filled else (whole, whole, TOKEN)),
    )(me, k, v, gk_in, gv_in, token, *later, *filled)


def even_half(me):
    return 1 - lax.rem(me, 2)


def odd_half(me):
    return lax.rem(me, 2)


def rows_of(array):
    return array.reshape(array.shape[1:])


def shards_four(queries, key_vectors, value_vectors, grad_output):
    out_shape = queries.shape
    q, k, v, g = (rows_of(x) for x in (queries, key_vectors, value_vectors, grad_output))
    me = lax.axis_index("ctx").astype(jnp.int32).reshape(1)
    token = jnp.zeros(TOKEN.shape, TOKEN.dtype)

    def send(x, pairs):
        return lax.ppermute(x, "ctx", pairs)

    s_a, s_kept, token = states((0, 1), (0,), me, k, v, token)
    r_a = send(s_a, [(0, 1)])
    s_b, token = states((1,), (1,), me, k, v, token, (0,), (s_kept,))
    r_b = send(s_b, [(1, 2)])
    s_c, token = near_states(0, (1, 2), me, k, v, token, (0,), (s_b,))
    r_c = send(s_c, [(0, 2), (2, 3)])
    intra_out, qt, token = intra(q, k, v, token)
    shared = (q, qt, g, intra_out)
    s12, token = add(token, r_a, s_c)
    r_far = send(s12, [(1, 3)])
    s_y, token, s12 = near_states(1, (2,), me, k, v, token, passed=(s12,))
    r_near = send(s12, [(0, 1), (1, 2)])
    r_b, token = add(token, r_b)
    s123, token = add(token, r_b, r_c, s_y)
    first, g_first, token = mid(even_half, (0, 1, 2), me, shared, token, (r_a, r_b, r_c))
    r_last = send(s123, [(2, 3)])
    first_end, g_one, token = mid(even_half, (3,), me, shared, token, (r_c, r_far), (2,), (g_first,))
    u_one = send(g_one, [(3, 2), (2, 1)])
    second, g_rest, token = mid(odd_half, (0, 1, 2), me, shared, token, (r_near,))
    second_end, g_two, g_second, token = mid(odd_half, (3,), me, shared, token, (r_last,), (1,), (g_first, g_rest))
    u_two = send(g_two, [(3, 1), (1, 0)])
    normed, grad_q, gk_second, gv_second, token = back(odd_half, (3,), me, q, k, v, token, (second, second_end))
    g12, token = add(token, u_one, g_second)
    w_far = send(g12, [(2, 0)])
    w_near = send(g12, [(3, 2), (2, 1)])
    g123, token = add(token, u_one, u_two, g_second)
    w_last = send(g123, [(1, 0)])
    normed, grad_q, gk_first, gv_first, token = back(
        even_half, (3,), me, q, k, v, token, (first, first_end), (normed, grad_q)
    )
    *filled, token = post(odd_half, me, k, v, gk_second, gv_second, token, (u_one, u_two, w_far))
    l_near, token = add(token, w_near)
    grad_k, grad_v = post(even_half, me, k, v, gk_first, gv_first, token, (l_near, w_last), filled)
    return tuple(x.reshape(out_shape) for x in (normed, grad_q, grad_k, grad_v))


def scan_states(first, second, count, backward):
    rows = first.shape[0] * 2
    shares = jnp.concatenate([first, second], axis=0).reshape(count, rows // count, DH)
    shares = lax.all_to_all(shares, "ctx", split_axis=0, concat_axis=0, tiled=True).astype(F32)
    running = jnp.cumsum(shares, axis=0)
    sums = running[-1:] - running if backward else running - shares
    sums = lax.all_to_all(sums.astype(BF16), "ctx", split_axis=0, concat_axis=0, tiled=True)
    sums = sums.reshape(rows, DH)
    return sums[: rows // 2], sums[rows // 2 :]


def low_half(me):
    return 0


def high_half(me):
    return 1


def shards_any(count, queries, key_vectors, value_vectors, grad_output):
    out_shape = queries.shape
    q, k, v, g = (rows_of(x) for x in (queries, key_vectors, value_vectors, grad_output))
    me = lax.axis_index("ctx").astype(jnp.int32).reshape(1)
    token = jnp.zeros(TOKEN.shape, TOKEN.dtype)
    s1, token = near_states(0, (), me, k, v, token)
    s2, token = near_states(1, (), me, k, v, token)
    e1, e2 = scan_states(s1, s2, count, False)
    intra_out, qt, token = intra(q, k, v, token)
    shared = (q, qt, g, intra_out)
    low, g1, token = mid(low_half, (), me, shared, token, (e1,))
    high, g2, token = mid(high_half, (), me, shared, token, (e2,))
    l1, l2 = scan_states(g1, g2, count, True)
    normed, grad_q, gk1, gv1, token = back(low_half, (), me, q, k, v, token, (low,))
    normed, grad_q, gk2, gv2, token = back(high_half, (), me, q, k, v, token, (high,), (normed, grad_q))
    *filled, token = post(low_half, me, k, v, gk1, gv1, token, (l1,))
    grad_k, grad_v = post(high_half, me, k, v, gk2, gv2, token, (l2,), filled)
    return tuple(x.reshape(out_shape) for x in (normed, grad_q, grad_k, grad_v))


def solution(mesh):
    placed = P(("groups", "dp"), "ctx", "tp")
    count = mesh.shape["ctx"]

    def shards(*args):
        if count == 4:
            return shards_four(*args)
        return shards_any(count, *args)

    return jax.shard_map(
        shards,
        mesh=mesh,
        in_specs=(placed,) * 4,
        out_specs=(placed,) * 4,
        check_vma=False,
    )
```

```python
import functools

import jax
import jax.numpy as jnp
from jax import lax
from jax.experimental import pallas as pl
from jax.experimental.pallas import tpu as pltpu
from jax.sharding import PartitionSpec as P

DH = 128
norm_eps = 1e-06
F32 = jnp.float32
BF16 = jnp.bfloat16

VMEM_SPEC = pl.BlockSpec(memory_space=pltpu.VMEM)
HBM_SPEC = pl.BlockSpec(memory_space=pltpu.HBM)
SMEM_SPEC = pl.BlockSpec(memory_space=pltpu.SMEM)
COST = pl.CostEstimate(flops=0, transcendentals=0, bytes_accessed=4096)
PARAMS = pltpu.CompilerParams(vmem_limit_bytes=16 << 20)


def params(name, parts):
    return dict(compiler_params=PARAMS, cost_estimate=COST, name=name, out_shape=parts)


def dot_nn(a, b):
    return lax.dot_general(a, b, (((1,), (0,)), ((), ())), preferred_element_type=F32)


def dot_nt(a, b):
    return lax.dot_general(a, b, (((1,), (1,)), ((), ())), preferred_element_type=F32)


def dot_tn(a, b):
    return lax.dot_general(a, b, (((0,), (0,)), ((), ())), preferred_element_type=F32)


def head(index):
    return slice(index * DH, (index + 1) * DH)


def causal(length):
    rows = lax.broadcasted_iota(jnp.int32, (length, length), 0)
    columns = lax.broadcasted_iota(jnp.int32, (length, length), 1)
    return columns <= rows


def half_columns(half, h, heads):
    return pl.ds(pl.multiple_of((half * heads + h) * DH, DH), DH)


def among(me, roles):
    hit = me == roles[0]
    for role in roles[1:]:
        hit = hit | (me == role)
    return hit


def on(me, roles):
    return pl.when(among(me, roles)) if roles else lambda body: body()


def near_state_kernel(half, roles, keep, me_ref, k_ref, v_ref, token_ref, *refs):
    passed = (len(refs) - 2 - len(keep)) // 2
    out_ref, done_ref, *copies = refs[-2 - passed :]
    heads = out_ref.shape[0] // DH
    done_ref[...] = token_ref[...]
    for source, copy in zip(refs[len(keep) :], copies):
        copy[...] = source[...]
    if keep:

        @on(me_ref[0], keep)
        def _():
            out_ref[...] = refs[0][...]

    @on(me_ref[0], roles)
    def _():
        for h in range(heads):
            cols = head(half * heads + h)
            out_ref[head(h), :] = dot_tn(k_ref[:, cols], v_ref[:, cols]).astype(BF16)


def near_states(half, roles, me, k, v, token, keep=(), spare=(), passed=()):
    shape = jax.ShapeDtypeStruct((k.shape[1] // 2, DH), BF16)
    return pl.pallas_call(
        functools.partial(near_state_kernel, half, roles, keep),
        in_specs=[SMEM_SPEC] + [VMEM_SPEC] * (3 + len(spare) + len(passed)),
        out_specs=(VMEM_SPEC,) * (2 + len(passed)),
        **params("near_states", (shape, TOKEN) + (shape,) * len(passed)),
    )(me, k, v, token, *spare, *passed)


def state_kernel(halves, roles, keep, me_ref, k_ref, v_ref, token_ref, *refs):
    done_ref, k_buf, v_buf, k_sem, v_sem = refs[-5:]
    outs = refs[len(keep) : -5]
    width = k_buf.shape[2]
    heads = width // DH
    done_ref[...] = token_ref[...]
    if keep:

        @on(me_ref[0], keep)
        def _():
            outs[0][...] = refs[0][...]

    @on(me_ref[0], roles)
    def _():
        copies = []
        for slot, half in enumerate(halves):
            cols = slice(half * width, (half + 1) * width)
            copies.append(pltpu.make_async_copy(k_ref.at[:, cols], k_buf.at[slot], k_sem.at[slot]))
            copies.append(pltpu.make_async_copy(v_ref.at[:, cols], v_buf.at[slot], v_sem.at[slot]))
        for copy in copies:
            copy.start()
        for copy in copies:
            copy.wait()
        for slot, out_ref in enumerate(outs):
            for h in range(heads):
                out_ref[head(h), :] = dot_tn(k_buf[slot, :, head(h)], v_buf[slot, :, head(h)]).astype(BF16)


def states(halves, roles, me, k, v, token, keep=(), spare=()):
    length, width = k.shape
    count = len(halves)
    k, v = (pltpu.with_memory_space_constraint(x, pltpu.HBM) for x in (k, v))
    shape = jax.ShapeDtypeStruct((width // 2, DH), BF16)
    return pl.pallas_call(
        functools.partial(state_kernel, halves, roles, keep),
        in_specs=[SMEM_SPEC, HBM_SPEC, HBM_SPEC] + [VMEM_SPEC] * (1 + len(spare)),
        out_specs=(VMEM_SPEC,) * (count + 1),
        scratch_shapes=[pltpu.VMEM((count, length, width // 2), BF16)] * 2 + [pltpu.SemaphoreType.DMA((count,))] * 2,
        **params("states", (shape,) * count + (TOKEN,)),
    )(me, k, v, token, *spare)


TOKEN = jax.ShapeDtypeStruct((8, DH), F32)


def intra_kernel(q_ref, k_ref, v_ref, token_ref, out_ref, qt_ref, done_ref):
    mask = causal(q_ref.shape[0])
    heads = q_ref.shape[1] // DH

    def scores_of(h):
        return jnp.where(mask, dot_nt(q_ref[:, head(h)], k_ref[:, head(h)]), 0.0).astype(BF16)

    scores = scores_of(0)
    for h in range(heads):
        ahead = scores_of(h + 1) if h + 1 < heads else None
        out_ref[:, head(h)] = dot_nn(scores, v_ref[:, head(h)])
        qt_ref[head(h), :] = q_ref[:, head(h)].T
        scores = ahead
    done_ref[...] = token_ref[...]


def intra(q, k, v, token):
    length, width = q.shape
    return pl.pallas_call(
        intra_kernel,
        in_specs=[VMEM_SPEC] * 4,
        out_specs=(VMEM_SPEC,) * 3,
        **params("intra", (jax.ShapeDtypeStruct(q.shape, F32), jax.ShapeDtypeStruct((width, length), BF16), TOKEN)),
    )(q, k, v, token)


def total(refs, rows=slice(None)):
    value = refs[0][rows, :].astype(F32)
    for ref in refs[1:]:
        value = value + ref[rows, :].astype(F32)
    return value.astype(BF16)


def add_kernel(token_ref, *refs):
    refs[-2][...] = total(refs[:-2])
    refs[-1][...] = token_ref[...]


def add(token, *arrays):
    return pl.pallas_call(
        add_kernel,
        in_specs=[VMEM_SPEC] * (1 + len(arrays)),
        out_specs=(VMEM_SPEC,) * 2,
        **params("add", (jax.ShapeDtypeStruct(arrays[0].shape, BF16), TOKEN)),
    )(token, *arrays)


def half_columns(half, h, heads):
    return pl.ds(pl.multiple_of((half * heads + h) * DH, DH), DH)


def half_copy(half, buf, ref, sem):
    width = buf.shape[1]
    return pltpu.make_async_copy(buf, ref.at[:, pl.ds(pl.multiple_of(half * width, width), width)], sem)


def mid_kernel(half_of, roles, keep, merge, me_ref, q_ref, qt_ref, g_ref, intra_ref, token_ref, *refs):
    normed_ref, grad_ref, earlier_ref, done_ref, *state_refs = refs[-5 - merge :]
    other, e_refs = refs[: len(keep) + merge], refs[len(keep) + merge : -5 - merge]
    state_ref = state_refs[0]
    heads = state_ref.shape[0] // DH
    done_ref[...] = token_ref[...]
    if keep:

        @on(me_ref[0], keep)
        def _():
            state_ref[...] = other[0][...]

    if merge:

        @pl.when(jnp.logical_not(among(me_ref[0], roles)))
        def _():
            state_refs[1][...] = other[-1][...]

    @on(me_ref[0], roles)
    def _():
        half = half_of(me_ref[0])
        cols = [half_columns(half, h, heads) for h in range(heads)]

        def mixed_of(h):
            earlier = total(e_refs, head(h))
            earlier_ref[head(h), :] = earlier
            return intra_ref[:, cols[h]] + dot_nn(q_ref[:, cols[h]], earlier)

        def put_state(h, grad):
            state = dot_nn(qt_ref[cols[h], :], grad).astype(BF16)
            for ref in state_refs:
                ref[head(h), :] = state

        mixed, last = mixed_of(0), None
        for h in range(heads):
            ahead = mixed_of(h + 1) if h + 1 < heads else None
            g = g_ref[:, cols[h]].astype(F32)
            squares = jnp.mean(mixed * mixed, axis=-1, keepdims=True)
            along = jnp.mean(g * mixed, axis=-1, keepdims=True)
            if h:
                put_state(h - 1, last)
            inverse = lax.rsqrt(squares + norm_eps)
            normed = mixed * inverse
            last = (inverse * (g - normed * (along * inverse))).astype(BF16)
            grad_ref[:, head(h)] = last
            normed_ref[:, head(h)] = normed.astype(BF16)
            mixed = ahead
        put_state(heads - 1, last)


def mid(half_of, roles, me, shared, token, earlier, keep=(), other=()):
    merge = len(other) - len(keep)
    length, width = shared[0].shape
    half_shape = jax.ShapeDtypeStruct((length, width // 2), BF16)
    state_shape = jax.ShapeDtypeStruct(earlier[0].shape, BF16)
    normed, grad, low, token, *states_out = pl.pallas_call(
        functools.partial(mid_kernel, half_of, roles, keep, merge),
        in_specs=[SMEM_SPEC] + [VMEM_SPEC] * (5 + len(other) + len(earlier)),
        out_specs=(VMEM_SPEC,) * (5 + merge),
        **params("mid", (half_shape, half_shape, state_shape, TOKEN) + (state_shape,) * (1 + merge)),
    )(me, *shared, token, *other, *earlier)
    return (normed, grad, low), *states_out, token


def back_kernel(half_of, roles, sets, me_ref, q_ref, k_ref, v_ref, token_ref, *refs):
    normed_ref, gq_ref, gk_ref, gv_ref, done_ref, gq_buf, n_buf, gq_sem, n_sem = refs[-9:]
    length = q_ref.shape[0]
    rows = lax.broadcasted_iota(jnp.int32, (length, length), 0)
    columns = lax.broadcasted_iota(jnp.int32, (length, length), 1)
    mask, mask_t = columns <= rows, rows <= columns
    heads = gk_ref.shape[1] // DH
    half = half_of(me_ref[0])

    def chosen(index, place):
        value = refs[index][place]
        if sets > 1:
            value = jnp.where(among(me_ref[0], roles), refs[3 + index][place], value)
        return value

    n_buf[...] = chosen(0, (slice(None), slice(None)))
    normed_copy = half_copy(half, n_buf, normed_ref, n_sem)
    normed_copy.start()
    for h in range(heads):
        cols = half_columns(half, h, heads)
        q, k, v = (ref[:, cols] for ref in (q_ref, k_ref, v_ref))
        grad = chosen(1, (slice(None), head(h)))
        earlier = chosen(2, (head(h), slice(None)))
        scores_t = jnp.where(mask_t, dot_nt(k, q), 0.0).astype(BF16)
        grad_scores = jnp.where(mask, dot_nt(grad, v), 0.0).astype(BF16)
        grad_scores_t = jnp.where(mask_t, dot_nt(v, grad), 0.0).astype(BF16)
        gq_buf[:, head(h)] = (dot_nn(grad_scores, k) + dot_nt(grad, earlier)).astype(BF16)
        gk_ref[:, head(h)] = dot_nn(grad_scores_t, q)
        gv_ref[:, head(h)] = dot_nn(scores_t, grad)
    done_ref[...] = token_ref[...]
    gq_copy = half_copy(half, gq_buf, gq_ref, gq_sem)
    gq_copy.start()
    normed_copy.wait()
    gq_copy.wait()


def back(half_of, roles, me, q, k, v, token, sets, filled=()):
    length, width = q.shape
    whole = jax.ShapeDtypeStruct(q.shape, BF16)
    half_shape = jax.ShapeDtypeStruct((length, width // 2), F32)
    first = 5 + 3 * len(sets)
    buffers = pltpu.VMEM((length, width // 2), BF16)
    return pl.pallas_call(
        functools.partial(back_kernel, half_of, roles, len(sets)),
        in_specs=[SMEM_SPEC] + [VMEM_SPEC] * (first - 1) + [HBM_SPEC] * len(filled),
        out_specs=(HBM_SPEC, HBM_SPEC, VMEM_SPEC, VMEM_SPEC, VMEM_SPEC),
        scratch_shapes=[buffers, buffers] + [pltpu.SemaphoreType.DMA] * 2,
        input_output_aliases={first: 0, first + 1: 1} if filled else {},
        **params("back", (whole, whole, half_shape, half_shape, TOKEN)),
    )(me, q, k, v, token, *(x for one in sets for x in one), *filled)


def post_first_kernel(half_of, parts, *refs):
    refs[-5][...] = refs[5][...]
    post_kernel(half_of, parts, *refs[:-5], *refs[-4:])


def post_kernel(half_of, parts, me_ref, k_ref, v_ref, gk_in_ref, gv_in_ref, token_ref, *refs):
    l_refs, (gk_ref, gv_ref, gk_buf, gv_buf, gk_sem, gv_sem) = refs[:parts], refs[-6:]
    heads = gk_in_ref.shape[1] // DH
    half = half_of(me_ref[0])
    laters = [total(l_refs, head(h)) for h in range(heads)]
    for h in range(heads):
        v = v_ref[:, half_columns(half, h, heads)]
        gk_buf[:, head(h)] = (gk_in_ref[:, head(h)] + dot_nt(v, laters[h])).astype(BF16)
    gk_copy = half_copy(half, gk_buf, gk_ref, gk_sem)
    gk_copy.start()
    for h in range(heads):
        k = k_ref[:, half_columns(half, h, heads)]
        gv_buf[:, head(h)] = (gv_in_ref[:, head(h)] + dot_nn(k, laters[h])).astype(BF16)
    gv_copy = half_copy(half, gv_buf, gv_ref, gv_sem)
    gv_copy.start()
    gk_copy.wait()
    gv_copy.wait()


def post(half_of, me, k, v, gk_in, gv_in, token, later, filled=()):
    length, width = k.shape
    first = 6 + len(later)
    whole = jax.ShapeDtypeStruct(k.shape, BF16)
    return pl.pallas_call(
        functools.partial(post_kernel if filled else post_first_kernel, half_of, len(later)),
        in_specs=[SMEM_SPEC] + [VMEM_SPEC] * (first - 1) + [HBM_SPEC] * len(filled),
        out_specs=(HBM_SPEC, HBM_SPEC) if filled else (HBM_SPEC, HBM_SPEC, VMEM_SPEC),
        scratch_shapes=[pltpu.VMEM((length, width // 2), BF16)] * 2 + [pltpu.SemaphoreType.DMA] * 2,
        input_output_aliases={first: 0, first + 1: 1} if filled else {},
        **params("post", (whole, whole) if filled else (whole, whole, TOKEN)),
    )(me, k, v, gk_in, gv_in, token, *later, *filled)


def even_half(me):
    return 1 - lax.rem(me, 2)


def odd_half(me):
    return lax.rem(me, 2)


def rows_of(array):
    return array.reshape(array.shape[1:])


def shards_four(queries, key_vectors, value_vectors, grad_output):
    out_shape = queries.shape
    q, k, v, g = (rows_of(x) for x in (queries, key_vectors, value_vectors, grad_output))
    me = lax.axis_index("ctx").astype(jnp.int32).reshape(1)
    token = jnp.zeros(TOKEN.shape, TOKEN.dtype)

    def send(x, pairs):
        return lax.ppermute(x, "ctx", pairs)

    s_a, s_kept, token = states((0, 1), (0,), me, k, v, token)
    r_a = send(s_a, [(0, 1)])
    s_b, token = states((1,), (1,), me, k, v, token, (0,), (s_kept,))
    r_b = send(s_b, [(1, 2)])
    s_c, token = near_states(0, (1, 2), me, k, v, token, (0,), (s_b,))
    r_c = send(s_c, [(0, 2), (2, 3)])
    intra_out, qt, token = intra(q, k, v, token)
    shared = (q, qt, g, intra_out)
    s12, token = add(token, r_a, s_c)
    r_far = send(s12, [(1, 3)])
    s_y, token, s12 = near_states(1, (2,), me, k, v, token, passed=(s12,))
    r_near = send(s12, [(0, 1), (1, 2)])
    r_b, token = add(token, r_b)
    s123, token = add(token, r_b, r_c, s_y)
    r_last = send(s123, [(2, 3)])
    first_end, g_one, token = mid(even_half, (3,), me, shared, token, (r_c, r_far))
    u_one = send(g_one, [(3, 2)])
    first, g_first, token = mid(even_half, (0, 1, 2), me, shared, token, (r_a, r_b, r_c))
    u_side = send(g_first, [(2, 1)])
    second, g_rest, token = mid(odd_half, (0, 1, 2), me, shared, token, (r_near,))
    second_end, g_two, g_second, token = mid(odd_half, (3,), me, shared, token, (r_last,), (1,), (g_first, g_rest))
    u_two = send(g_two, [(3, 1), (1, 0)])
    normed, grad_q, gk_second, gv_second, token = back(odd_half, (3,), me, q, k, v, token, (second, second_end))
    g12, token = add(token, u_one, g_second)
    w_far = send(g12, [(2, 0)])
    w_near = send(g12, [(3, 2), (2, 1)])
    g123, token = add(token, u_side, u_two, g_second)
    w_last = send(g123, [(1, 0)])
    normed, grad_q, gk_first, gv_first, token = back(
        even_half, (3,), me, q, k, v, token, (first, first_end), (normed, grad_q)
    )
    *filled, token = post(odd_half, me, k, v, gk_second, gv_second, token, (u_one, u_side, u_two, w_far))
    l_near, token = add(token, w_near)
    grad_k, grad_v = post(even_half, me, k, v, gk_first, gv_first, token, (l_near, w_last), filled)
    return tuple(x.reshape(out_shape) for x in (normed, grad_q, grad_k, grad_v))


def scan_states(first, second, count, backward):
    rows = first.shape[0] * 2
    shares = jnp.concatenate([first, second], axis=0).reshape(count, rows // count, DH)
    shares = lax.all_to_all(shares, "ctx", split_axis=0, concat_axis=0, tiled=True).astype(F32)
    running = jnp.cumsum(shares, axis=0)
    sums = running[-1:] - running if backward else running - shares
    sums = lax.all_to_all(sums.astype(BF16), "ctx", split_axis=0, concat_axis=0, tiled=True)
    sums = sums.reshape(rows, DH)
    return sums[: rows // 2], sums[rows // 2 :]


def low_half(me):
    return 0


def high_half(me):
    return 1


def shards_any(count, queries, key_vectors, value_vectors, grad_output):
    out_shape = queries.shape
    q, k, v, g = (rows_of(x) for x in (queries, key_vectors, value_vectors, grad_output))
    me = lax.axis_index("ctx").astype(jnp.int32).reshape(1)
    token = jnp.zeros(TOKEN.shape, TOKEN.dtype)
    s1, token = near_states(0, (), me, k, v, token)
    s2, token = near_states(1, (), me, k, v, token)
    e1, e2 = scan_states(s1, s2, count, False)
    intra_out, qt, token = intra(q, k, v, token)
    shared = (q, qt, g, intra_out)
    low, g1, token = mid(low_half, (), me, shared, token, (e1,))
    high, g2, token = mid(high_half, (), me, shared, token, (e2,))
    l1, l2 = scan_states(g1, g2, count, True)
    normed, grad_q, gk1, gv1, token = back(low_half, (), me, q, k, v, token, (low,))
    normed, grad_q, gk2, gv2, token = back(high_half, (), me, q, k, v, token, (high,), (normed, grad_q))
    *filled, token = post(low_half, me, k, v, gk1, gv1, token, (l1,))
    grad_k, grad_v = post(high_half, me, k, v, gk2, gv2, token, (l2,), filled)
    return tuple(x.reshape(out_shape) for x in (normed, grad_q, grad_k, grad_v))


def solution(mesh):
    placed = P(("groups", "dp"), "ctx", "tp")
    count = mesh.shape["ctx"]

    def shards(*args):
        if count == 4:
            return shards_four(*args)
        return shards_any(count, *args)

    return jax.shard_map(
        shards,
        mesh=mesh,
        in_specs=(placed,) * 4,
        out_specs=(placed,) * 4,
        check_vma=False,
    )
```

```python
import functools

import jax
import jax.numpy as jnp
from jax import lax
from jax.experimental import pallas as pl
from jax.experimental.pallas import tpu as pltpu
from jax.sharding import PartitionSpec as P

DH = 128
norm_eps = 1e-06
F32 = jnp.float32
BF16 = jnp.bfloat16

VMEM_SPEC = pl.BlockSpec(memory_space=pltpu.VMEM)
HBM_SPEC = pl.BlockSpec(memory_space=pltpu.HBM)
SMEM_SPEC = pl.BlockSpec(memory_space=pltpu.SMEM)
COST = pl.CostEstimate(flops=0, transcendentals=0, bytes_accessed=4096)
PARAMS = pltpu.CompilerParams(vmem_limit_bytes=16 << 20)


def params(name, parts):
    return dict(compiler_params=PARAMS, cost_estimate=COST, name=name, out_shape=parts)


def dot_nn(a, b):
    return lax.dot_general(a, b, (((1,), (0,)), ((), ())), preferred_element_type=F32)


def dot_nt(a, b):
    return lax.dot_general(a, b, (((1,), (1,)), ((), ())), preferred_element_type=F32)


def dot_tn(a, b):
    return lax.dot_general(a, b, (((0,), (0,)), ((), ())), preferred_element_type=F32)


def head(index):
    return slice(index * DH, (index + 1) * DH)


def causal(length):
    rows = lax.broadcasted_iota(jnp.int32, (length, length), 0)
    columns = lax.broadcasted_iota(jnp.int32, (length, length), 1)
    return columns <= rows


def half_columns(half, h, heads):
    return pl.ds(pl.multiple_of((half * heads + h) * DH, DH), DH)


def among(me, roles):
    hit = me == roles[0]
    for role in roles[1:]:
        hit = hit | (me == role)
    return hit


def on(me, roles):
    return pl.when(among(me, roles)) if roles else lambda body: body()


def near_state_kernel(half, roles, keep, me_ref, k_ref, v_ref, token_ref, *refs):
    passed = (len(refs) - 2 - len(keep)) // 2
    out_ref, done_ref, *copies = refs[-2 - passed :]
    heads = out_ref.shape[0] // DH
    done_ref[...] = token_ref[...]
    for source, copy in zip(refs[len(keep) :], copies):
        copy[...] = source[...]
    if keep:

        @on(me_ref[0], keep)
        def _():
            out_ref[...] = refs[0][...]

    @on(me_ref[0], roles)
    def _():
        for h in range(heads):
            cols = head(half * heads + h)
            out_ref[head(h), :] = dot_tn(k_ref[:, cols], v_ref[:, cols]).astype(BF16)


def near_states(half, roles, me, k, v, token, keep=(), spare=(), passed=()):
    shape = jax.ShapeDtypeStruct((k.shape[1] // 2, DH), BF16)
    return pl.pallas_call(
        functools.partial(near_state_kernel, half, roles, keep),
        in_specs=[SMEM_SPEC] + [VMEM_SPEC] * (3 + len(spare) + len(passed)),
        out_specs=(VMEM_SPEC,) * (2 + len(passed)),
        **params("near_states", (shape, TOKEN) + (shape,) * len(passed)),
    )(me, k, v, token, *spare, *passed)


def state_kernel(halves, roles, keep, me_ref, k_ref, v_ref, token_ref, *refs):
    done_ref, k_buf, v_buf, k_sem, v_sem = refs[-5:]
    outs = refs[len(keep) : -5]
    width = k_buf.shape[2]
    heads = width // DH
    done_ref[...] = token_ref[...]
    if keep:

        @on(me_ref[0], keep)
        def _():
            outs[0][...] = refs[0][...]

    @on(me_ref[0], roles)
    def _():
        copies = []
        for slot, half in enumerate(halves):
            cols = slice(half * width, (half + 1) * width)
            copies.append(pltpu.make_async_copy(k_ref.at[:, cols], k_buf.at[slot], k_sem.at[slot]))
            copies.append(pltpu.make_async_copy(v_ref.at[:, cols], v_buf.at[slot], v_sem.at[slot]))
        for copy in copies:
            copy.start()
        for copy in copies:
            copy.wait()
        for slot, out_ref in enumerate(outs):
            for h in range(heads):
                out_ref[head(h), :] = dot_tn(k_buf[slot, :, head(h)], v_buf[slot, :, head(h)]).astype(BF16)


def states(halves, roles, me, k, v, token, keep=(), spare=()):
    length, width = k.shape
    count = len(halves)
    k, v = (pltpu.with_memory_space_constraint(x, pltpu.HBM) for x in (k, v))
    shape = jax.ShapeDtypeStruct((width // 2, DH), BF16)
    return pl.pallas_call(
        functools.partial(state_kernel, halves, roles, keep),
        in_specs=[SMEM_SPEC, HBM_SPEC, HBM_SPEC] + [VMEM_SPEC] * (1 + len(spare)),
        out_specs=(VMEM_SPEC,) * (count + 1),
        scratch_shapes=[pltpu.VMEM((count, length, width // 2), BF16)] * 2 + [pltpu.SemaphoreType.DMA((count,))] * 2,
        **params("states", (shape,) * count + (TOKEN,)),
    )(me, k, v, token, *spare)


TOKEN = jax.ShapeDtypeStruct((8, DH), F32)


def intra_kernel(q_ref, k_ref, v_ref, token_ref, out_ref, qt_ref, done_ref):
    mask = causal(q_ref.shape[0])
    heads = q_ref.shape[1] // DH

    def scores_of(h):
        return jnp.where(mask, dot_nt(q_ref[:, head(h)], k_ref[:, head(h)]), 0.0).astype(BF16)

    scores = scores_of(0)
    for h in range(heads):
        ahead = scores_of(h + 1) if h + 1 < heads else None
        out_ref[:, head(h)] = dot_nn(scores, v_ref[:, head(h)])
        qt_ref[head(h), :] = q_ref[:, head(h)].T
        scores = ahead
    done_ref[...] = token_ref[...]


def intra(q, k, v, token):
    length, width = q.shape
    return pl.pallas_call(
        intra_kernel,
        in_specs=[VMEM_SPEC] * 4,
        out_specs=(VMEM_SPEC,) * 3,
        **params("intra", (jax.ShapeDtypeStruct(q.shape, F32), jax.ShapeDtypeStruct((width, length), BF16), TOKEN)),
    )(q, k, v, token)


def total(refs, rows=slice(None)):
    value = refs[0][rows, :].astype(F32)
    for ref in refs[1:]:
        value = value + ref[rows, :].astype(F32)
    return value.astype(BF16)


def add_kernel(token_ref, *refs):
    refs[-2][...] = total(refs[:-2])
    refs[-1][...] = token_ref[...]


def add(token, *arrays):
    return pl.pallas_call(
        add_kernel,
        in_specs=[VMEM_SPEC] * (1 + len(arrays)),
        out_specs=(VMEM_SPEC,) * 2,
        **params("add", (jax.ShapeDtypeStruct(arrays[0].shape, BF16), TOKEN)),
    )(token, *arrays)


def half_columns(half, h, heads):
    return pl.ds(pl.multiple_of((half * heads + h) * DH, DH), DH)


def half_copy(half, buf, ref, sem):
    width = buf.shape[1]
    return pltpu.make_async_copy(buf, ref.at[:, pl.ds(pl.multiple_of(half * width, width), width)], sem)


def mid_kernel(half_of, roles, keep, merge, me_ref, q_ref, qt_ref, g_ref, intra_ref, token_ref, *refs):
    normed_ref, grad_ref, earlier_ref, done_ref, *state_refs = refs[-5 - merge :]
    other, e_refs = refs[: len(keep) + merge], refs[len(keep) + merge : -5 - merge]
    state_ref = state_refs[0]
    heads = state_ref.shape[0] // DH
    done_ref[...] = token_ref[...]
    if keep:

        @on(me_ref[0], keep)
        def _():
            state_ref[...] = other[0][...]

    if merge:

        @pl.when(jnp.logical_not(among(me_ref[0], roles)))
        def _():
            state_refs[1][...] = other[-1][...]

    @on(me_ref[0], roles)
    def _():
        half = half_of(me_ref[0])
        cols = [half_columns(half, h, heads) for h in range(heads)]

        def mixed_of(h):
            earlier = total(e_refs, head(h))
            earlier_ref[head(h), :] = earlier
            return intra_ref[:, cols[h]] + dot_nn(q_ref[:, cols[h]], earlier)

        def put_state(h, grad):
            state = dot_nn(qt_ref[cols[h], :], grad).astype(BF16)
            for ref in state_refs:
                ref[head(h), :] = state

        mixed, last = mixed_of(0), None
        for h in range(heads):
            ahead = mixed_of(h + 1) if h + 1 < heads else None
            g = g_ref[:, cols[h]].astype(F32)
            squares = jnp.mean(mixed * mixed, axis=-1, keepdims=True)
            along = jnp.mean(g * mixed, axis=-1, keepdims=True)
            if h:
                put_state(h - 1, last)
            inverse = lax.rsqrt(squares + norm_eps)
            normed = mixed * inverse
            last = (inverse * (g - normed * (along * inverse))).astype(BF16)
            grad_ref[:, head(h)] = last
            normed_ref[:, head(h)] = normed.astype(BF16)
            mixed = ahead
        put_state(heads - 1, last)


def mid(half_of, roles, me, shared, token, earlier, keep=(), other=()):
    merge = len(other) - len(keep)
    length, width = shared[0].shape
    half_shape = jax.ShapeDtypeStruct((length, width // 2), BF16)
    state_shape = jax.ShapeDtypeStruct(earlier[0].shape, BF16)
    normed, grad, low, token, *states_out = pl.pallas_call(
        functools.partial(mid_kernel, half_of, roles, keep, merge),
        in_specs=[SMEM_SPEC] + [VMEM_SPEC] * (5 + len(other) + len(earlier)),
        out_specs=(VMEM_SPEC,) * (5 + merge),
        **params("mid", (half_shape, half_shape, state_shape, TOKEN) + (state_shape,) * (1 + merge)),
    )(me, *shared, token, *other, *earlier)
    return (normed, grad, low), *states_out, token


def back_kernel(half_of, roles, sets, me_ref, q_ref, k_ref, v_ref, token_ref, *refs):
    normed_ref, gq_ref, gk_ref, gv_ref, done_ref, gq_buf, n_buf, gq_sem, n_sem = refs[-9:]
    length = q_ref.shape[0]
    rows = lax.broadcasted_iota(jnp.int32, (length, length), 0)
    columns = lax.broadcasted_iota(jnp.int32, (length, length), 1)
    mask, mask_t = columns <= rows, rows <= columns
    heads = gk_ref.shape[1] // DH
    half = half_of(me_ref[0])

    def chosen(index, place):
        value = refs[index][place]
        if sets > 1:
            value = jnp.where(among(me_ref[0], roles), refs[3 + index][place], value)
        return value

    n_buf[...] = chosen(0, (slice(None), slice(None)))
    normed_copy = half_copy(half, n_buf, normed_ref, n_sem)
    normed_copy.start()
    for h in range(heads):
        cols = half_columns(half, h, heads)
        q, k, v = (ref[:, cols] for ref in (q_ref, k_ref, v_ref))
        grad = chosen(1, (slice(None), head(h)))
        earlier = chosen(2, (head(h), slice(None)))
        scores_t = jnp.where(mask_t, dot_nt(k, q), 0.0).astype(BF16)
        grad_scores = jnp.where(mask, dot_nt(grad, v), 0.0).astype(BF16)
        grad_scores_t = jnp.where(mask_t, dot_nt(v, grad), 0.0).astype(BF16)
        gq_buf[:, head(h)] = (dot_nn(grad_scores, k) + dot_nt(grad, earlier)).astype(BF16)
        gk_ref[:, head(h)] = dot_nn(grad_scores_t, q)
        gv_ref[:, head(h)] = dot_nn(scores_t, grad)
    done_ref[...] = token_ref[...]
    gq_copy = half_copy(half, gq_buf, gq_ref, gq_sem)
    gq_copy.start()
    normed_copy.wait()
    gq_copy.wait()


def back(half_of, roles, me, q, k, v, token, sets, filled=()):
    length, width = q.shape
    whole = jax.ShapeDtypeStruct(q.shape, BF16)
    half_shape = jax.ShapeDtypeStruct((length, width // 2), F32)
    first = 5 + 3 * len(sets)
    buffers = pltpu.VMEM((length, width // 2), BF16)
    return pl.pallas_call(
        functools.partial(back_kernel, half_of, roles, len(sets)),
        in_specs=[SMEM_SPEC] + [VMEM_SPEC] * (first - 1) + [HBM_SPEC] * len(filled),
        out_specs=(HBM_SPEC, HBM_SPEC, VMEM_SPEC, VMEM_SPEC, VMEM_SPEC),
        scratch_shapes=[buffers, buffers] + [pltpu.SemaphoreType.DMA] * 2,
        input_output_aliases={first: 0, first + 1: 1} if filled else {},
        **params("back", (whole, whole, half_shape, half_shape, TOKEN)),
    )(me, q, k, v, token, *(x for one in sets for x in one), *filled)


def post_first_kernel(half_of, parts, *refs):
    refs[-5][...] = refs[5][...]
    post_kernel(half_of, parts, *refs[:-5], *refs[-4:])


def post_kernel(half_of, parts, me_ref, k_ref, v_ref, gk_in_ref, gv_in_ref, token_ref, *refs):
    l_refs, (gk_ref, gv_ref, gk_buf, gv_buf, gk_sem, gv_sem) = refs[:parts], refs[-6:]
    heads = gk_in_ref.shape[1] // DH
    half = half_of(me_ref[0])
    laters = [total(l_refs, head(h)) for h in range(heads)]
    for h in range(heads):
        k = k_ref[:, half_columns(half, h, heads)]
        gv_buf[:, head(h)] = (gv_in_ref[:, head(h)] + dot_nn(k, laters[h])).astype(BF16)
    gv_copy = half_copy(half, gv_buf, gv_ref, gv_sem)
    gv_copy.start()
    for h in range(heads):
        v = v_ref[:, half_columns(half, h, heads)]
        gk_buf[:, head(h)] = (gk_in_ref[:, head(h)] + dot_nt(v, laters[h])).astype(BF16)
    gk_copy = half_copy(half, gk_buf, gk_ref, gk_sem)
    gk_copy.start()
    gk_copy.wait()
    gv_copy.wait()


def post(half_of, me, k, v, gk_in, gv_in, token, later, filled=()):
    length, width = k.shape
    first = 6 + len(later)
    whole = jax.ShapeDtypeStruct(k.shape, BF16)
    return pl.pallas_call(
        functools.partial(post_kernel if filled else post_first_kernel, half_of, len(later)),
        in_specs=[SMEM_SPEC] + [VMEM_SPEC] * (first - 1) + [HBM_SPEC] * len(filled),
        out_specs=(HBM_SPEC, HBM_SPEC) if filled else (HBM_SPEC, HBM_SPEC, VMEM_SPEC),
        scratch_shapes=[pltpu.VMEM((length, width // 2), BF16)] * 2 + [pltpu.SemaphoreType.DMA] * 2,
        input_output_aliases={first: 0, first + 1: 1} if filled else {},
        **params("post", (whole, whole) if filled else (whole, whole, TOKEN)),
    )(me, k, v, gk_in, gv_in, token, *later, *filled)


def even_half(me):
    return 1 - lax.rem(me, 2)


def odd_half(me):
    return lax.rem(me, 2)


def rows_of(array):
    return array.reshape(array.shape[1:])


def shards_four(queries, key_vectors, value_vectors, grad_output):
    out_shape = queries.shape
    q, k, v, g = (rows_of(x) for x in (queries, key_vectors, value_vectors, grad_output))
    me = lax.axis_index("ctx").astype(jnp.int32).reshape(1)
    token = jnp.zeros(TOKEN.shape, TOKEN.dtype)

    def send(x, pairs):
        return lax.ppermute(x, "ctx", pairs)

    s_a, s_kept, token = states((0, 1), (0,), me, k, v, token)
    r_a = send(s_a, [(0, 1)])
    s_b, token = states((1,), (1,), me, k, v, token, (0,), (s_kept,))
    r_b = send(s_b, [(1, 2)])
    s_c, token = near_states(0, (1, 2), me, k, v, token, (0,), (s_b,))
    r_c = send(s_c, [(0, 2), (2, 3)])
    intra_out, qt, token = intra(q, k, v, token)
    shared = (q, qt, g, intra_out)
    s12, token = add(token, r_a, s_c)
    r_far = send(s12, [(1, 3)])
    s_y, token, s12 = near_states(1, (2,), me, k, v, token, passed=(s12,))
    r_near = send(s12, [(0, 1), (1, 2)])
    r_b, token = add(token, r_b)
    s123, token = add(token, r_b, r_c, s_y)
    first, g_first, token = mid(even_half, (0, 1, 2), me, shared, token, (r_a, r_b, r_c))
    r_last = send(s123, [(2, 3)])
    first_end, g_one, token = mid(even_half, (3,), me, shared, token, (r_c, r_far), (2,), (g_first,))
    u_one = send(g_one, [(3, 2), (2, 1)])
    second, g_rest, token = mid(odd_half, (0, 1, 2), me, shared, token, (r_near,))
    second_end, g_two, g_second, token = mid(odd_half, (3,), me, shared, token, (r_last,), (1,), (g_first, g_rest))
    u_two = send(g_two, [(3, 1), (1, 0)])
    normed, grad_q, gk_second, gv_second, token = back(odd_half, (3,), me, q, k, v, token, (second, second_end))
    g12, token = add(token, u_one, g_second)
    w_far = send(g12, [(2, 0)])
    w_near = send(g12, [(3, 2), (2, 1)])
    g123, token = add(token, u_one, u_two, g_second)
    w_last = send(g123, [(1, 0)])
    normed, grad_q, gk_first, gv_first, token = back(
        even_half, (3,), me, q, k, v, token, (first, first_end), (normed, grad_q)
    )
    *filled, token = post(odd_half, me, k, v, gk_second, gv_second, token, (u_one, u_two, w_far))
    l_near, token = add(token, w_near)
    grad_k, grad_v = post(even_half, me, k, v, gk_first, gv_first, token, (l_near, w_last), filled)
    return tuple(x.reshape(out_shape) for x in (normed, grad_q, grad_k, grad_v))


def scan_states(first, second, count, backward):
    rows = first.shape[0] * 2
    shares = jnp.concatenate([first, second], axis=0).reshape(count, rows // count, DH)
    shares = lax.all_to_all(shares, "ctx", split_axis=0, concat_axis=0, tiled=True).astype(F32)
    running = jnp.cumsum(shares, axis=0)
    sums = running[-1:] - running if backward else running - shares
    sums = lax.all_to_all(sums.astype(BF16), "ctx", split_axis=0, concat_axis=0, tiled=True)
    sums = sums.reshape(rows, DH)
    return sums[: rows // 2], sums[rows // 2 :]


def low_half(me):
    return 0


def high_half(me):
    return 1


def shards_any(count, queries, key_vectors, value_vectors, grad_output):
    out_shape = queries.shape
    q, k, v, g = (rows_of(x) for x in (queries, key_vectors, value_vectors, grad_output))
    me = lax.axis_index("ctx").astype(jnp.int32).reshape(1)
    token = jnp.zeros(TOKEN.shape, TOKEN.dtype)
    s1, token = near_states(0, (), me, k, v, token)
    s2, token = near_states(1, (), me, k, v, token)
    e1, e2 = scan_states(s1, s2, count, False)
    intra_out, qt, token = intra(q, k, v, token)
    shared = (q, qt, g, intra_out)
    low, g1, token = mid(low_half, (), me, shared, token, (e1,))
    high, g2, token = mid(high_half, (), me, shared, token, (e2,))
    l1, l2 = scan_states(g1, g2, count, True)
    normed, grad_q, gk1, gv1, token = back(low_half, (), me, q, k, v, token, (low,))
    normed, grad_q, gk2, gv2, token = back(high_half, (), me, q, k, v, token, (high,), (normed, grad_q))
    *filled, token = post(low_half, me, k, v, gk1, gv1, token, (l1,))
    grad_k, grad_v = post(high_half, me, k, v, gk2, gv2, token, (l2,), filled)
    return tuple(x.reshape(out_shape) for x in (normed, grad_q, grad_k, grad_v))


def solution(mesh):
    placed = P(("groups", "dp"), "ctx", "tp")
    count = mesh.shape["ctx"]

    def shards(*args):
        if count == 4:
            return shards_four(*args)
        return shards_any(count, *args)

    return jax.shard_map(
        shards,
        mesh=mesh,
        in_specs=(placed,) * 4,
        out_specs=(placed,) * 4,
        check_vma=False,
    )
```

```python
import functools

import jax
import jax.numpy as jnp
from jax import lax
from jax.experimental import pallas as pl
from jax.experimental.pallas import tpu as pltpu
from jax.sharding import PartitionSpec as P

DH = 128
norm_eps = 1e-06
F32 = jnp.float32
BF16 = jnp.bfloat16

VMEM_SPEC = pl.BlockSpec(memory_space=pltpu.VMEM)
HBM_SPEC = pl.BlockSpec(memory_space=pltpu.HBM)
SMEM_SPEC = pl.BlockSpec(memory_space=pltpu.SMEM)
COST = pl.CostEstimate(flops=0, transcendentals=0, bytes_accessed=4096)
PARAMS = pltpu.CompilerParams(vmem_limit_bytes=16 << 20)


def params(name, parts):
    return dict(compiler_params=PARAMS, cost_estimate=COST, name=name, out_shape=parts)


def dot_nn(a, b):
    return lax.dot_general(a, b, (((1,), (0,)), ((), ())), preferred_element_type=F32)


def dot_nt(a, b):
    return lax.dot_general(a, b, (((1,), (1,)), ((), ())), preferred_element_type=F32)


def dot_tn(a, b):
    return lax.dot_general(a, b, (((0,), (0,)), ((), ())), preferred_element_type=F32)


def head(index):
    return slice(index * DH, (index + 1) * DH)


def causal(length):
    rows = lax.broadcasted_iota(jnp.int32, (length, length), 0)
    columns = lax.broadcasted_iota(jnp.int32, (length, length), 1)
    return columns <= rows


def half_columns(half, h, heads):
    return pl.ds(pl.multiple_of((half * heads + h) * DH, DH), DH)


def among(me, roles):
    hit = me == roles[0]
    for role in roles[1:]:
        hit = hit | (me == role)
    return hit


def on(me, roles):
    return pl.when(among(me, roles)) if roles else lambda body: body()


def near_state_kernel(half, roles, keep, me_ref, k_ref, v_ref, token_ref, *refs):
    passed = (len(refs) - 2 - len(keep)) // 2
    out_ref, done_ref, *copies = refs[-2 - passed :]
    heads = out_ref.shape[0] // DH
    done_ref[...] = token_ref[...]
    for source, copy in zip(refs[len(keep) :], copies):
        copy[...] = source[...]
    if keep:

        @on(me_ref[0], keep)
        def _():
            out_ref[...] = refs[0][...]

    @on(me_ref[0], roles)
    def _():
        for h in range(heads):
            cols = head(half * heads + h)
            out_ref[head(h), :] = dot_tn(k_ref[:, cols], v_ref[:, cols]).astype(BF16)


def near_states(half, roles, me, k, v, token, keep=(), spare=(), passed=()):
    shape = jax.ShapeDtypeStruct((k.shape[1] // 2, DH), BF16)
    return pl.pallas_call(
        functools.partial(near_state_kernel, half, roles, keep),
        in_specs=[SMEM_SPEC] + [VMEM_SPEC] * (3 + len(spare) + len(passed)),
        out_specs=(VMEM_SPEC,) * (2 + len(passed)),
        **params("near_states", (shape, TOKEN) + (shape,) * len(passed)),
    )(me, k, v, token, *spare, *passed)


def state_kernel(halves, roles, keep, me_ref, k_ref, v_ref, token_ref, *refs):
    done_ref, k_buf, v_buf, k_sem, v_sem = refs[-5:]
    outs = refs[len(keep) : -5]
    width = k_buf.shape[2]
    heads = width // DH
    done_ref[...] = token_ref[...]
    if keep:

        @on(me_ref[0], keep)
        def _():
            outs[0][...] = refs[0][...]

    @on(me_ref[0], roles)
    def _():
        copies = []
        for slot, half in enumerate(halves):
            cols = slice(half * width, (half + 1) * width)
            copies.append(pltpu.make_async_copy(k_ref.at[:, cols], k_buf.at[slot], k_sem.at[slot]))
            copies.append(pltpu.make_async_copy(v_ref.at[:, cols], v_buf.at[slot], v_sem.at[slot]))
        for copy in copies:
            copy.start()
        for copy in copies:
            copy.wait()
        for slot, out_ref in enumerate(outs):
            for h in range(heads):
                out_ref[head(h), :] = dot_tn(k_buf[slot, :, head(h)], v_buf[slot, :, head(h)]).astype(BF16)


def states(halves, roles, me, k, v, token, keep=(), spare=()):
    length, width = k.shape
    count = len(halves)
    k, v = (pltpu.with_memory_space_constraint(x, pltpu.HBM) for x in (k, v))
    shape = jax.ShapeDtypeStruct((width // 2, DH), BF16)
    return pl.pallas_call(
        functools.partial(state_kernel, halves, roles, keep),
        in_specs=[SMEM_SPEC, HBM_SPEC, HBM_SPEC] + [VMEM_SPEC] * (1 + len(spare)),
        out_specs=(VMEM_SPEC,) * (count + 1),
        scratch_shapes=[pltpu.VMEM((count, length, width // 2), BF16)] * 2 + [pltpu.SemaphoreType.DMA((count,))] * 2,
        **params("states", (shape,) * count + (TOKEN,)),
    )(me, k, v, token, *spare)


TOKEN = jax.ShapeDtypeStruct((8, DH), F32)


def intra_kernel(q_ref, k_ref, v_ref, token_ref, out_ref, qt_ref, done_ref):
    mask = causal(q_ref.shape[0])
    heads = q_ref.shape[1] // DH

    def scores_of(h):
        return jnp.where(mask, dot_nt(q_ref[:, head(h)], k_ref[:, head(h)]), 0.0).astype(BF16)

    scores = scores_of(0)
    for h in range(heads):
        ahead = scores_of(h + 1) if h + 1 < heads else None
        out_ref[:, head(h)] = dot_nn(scores, v_ref[:, head(h)])
        qt_ref[head(h), :] = q_ref[:, head(h)].T
        scores = ahead
    done_ref[...] = token_ref[...]


def intra(q, k, v, token):
    length, width = q.shape
    return pl.pallas_call(
        intra_kernel,
        in_specs=[VMEM_SPEC] * 4,
        out_specs=(VMEM_SPEC,) * 3,
        **params("intra", (jax.ShapeDtypeStruct(q.shape, F32), jax.ShapeDtypeStruct((width, length), BF16), TOKEN)),
    )(q, k, v, token)


def total(refs, rows=slice(None)):
    value = refs[0][rows, :].astype(F32)
    for ref in refs[1:]:
        value = value + ref[rows, :].astype(F32)
    return value.astype(BF16)


def add_kernel(token_ref, *refs):
    refs[-2][...] = total(refs[:-2])
    refs[-1][...] = token_ref[...]


def add(token, *arrays):
    return pl.pallas_call(
        add_kernel,
        in_specs=[VMEM_SPEC] * (1 + len(arrays)),
        out_specs=(VMEM_SPEC,) * 2,
        **params("add", (jax.ShapeDtypeStruct(arrays[0].shape, BF16), TOKEN)),
    )(token, *arrays)


def half_columns(half, h, heads):
    return pl.ds(pl.multiple_of((half * heads + h) * DH, DH), DH)


def half_copy(half, buf, ref, sem):
    width = buf.shape[1]
    return pltpu.make_async_copy(buf, ref.at[:, pl.ds(pl.multiple_of(half * width, width), width)], sem)


def mid_kernel(half_of, roles, keep, merge, me_ref, q_ref, qt_ref, g_ref, intra_ref, token_ref, *refs):
    normed_ref, grad_ref, earlier_ref, done_ref, *state_refs = refs[-5 - merge :]
    other, e_refs = refs[: len(keep) + merge], refs[len(keep) + merge : -5 - merge]
    state_ref = state_refs[0]
    heads = state_ref.shape[0] // DH
    done_ref[...] = token_ref[...]
    if keep:

        @on(me_ref[0], keep)
        def _():
            state_ref[...] = other[0][...]

    if merge:

        @pl.when(jnp.logical_not(among(me_ref[0], roles)))
        def _():
            state_refs[1][...] = other[-1][...]

    @on(me_ref[0], roles)
    def _():
        half = half_of(me_ref[0])
        cols = [half_columns(half, h, heads) for h in range(heads)]

        def mixed_of(h):
            earlier = total(e_refs, head(h))
            earlier_ref[head(h), :] = earlier
            return intra_ref[:, cols[h]] + dot_nn(q_ref[:, cols[h]], earlier)

        def put_state(h, grad):
            state = dot_nn(qt_ref[cols[h], :], grad).astype(BF16)
            for ref in state_refs:
                ref[head(h), :] = state

        mixed, last = mixed_of(0), None
        for h in range(heads):
            ahead = mixed_of(h + 1) if h + 1 < heads else None
            g = g_ref[:, cols[h]].astype(F32)
            squares = jnp.mean(mixed * mixed, axis=-1, keepdims=True)
            along = jnp.mean(g * mixed, axis=-1, keepdims=True)
            if h:
                put_state(h - 1, last)
            inverse = lax.rsqrt(squares + norm_eps)
            normed = mixed * inverse
            last = (inverse * (g - normed * (along * inverse))).astype(BF16)
            grad_ref[:, head(h)] = last
            normed_ref[:, head(h)] = normed.astype(BF16)
            mixed = ahead
        put_state(heads - 1, last)


def mid(half_of, roles, me, shared, token, earlier, keep=(), other=()):
    merge = len(other) - len(keep)
    length, width = shared[0].shape
    half_shape = jax.ShapeDtypeStruct((length, width // 2), BF16)
    state_shape = jax.ShapeDtypeStruct(earlier[0].shape, BF16)
    normed, grad, low, token, *states_out = pl.pallas_call(
        functools.partial(mid_kernel, half_of, roles, keep, merge),
        in_specs=[SMEM_SPEC] + [VMEM_SPEC] * (5 + len(other) + len(earlier)),
        out_specs=(VMEM_SPEC,) * (5 + merge),
        **params("mid", (half_shape, half_shape, state_shape, TOKEN) + (state_shape,) * (1 + merge)),
    )(me, *shared, token, *other, *earlier)
    return (normed, grad, low), *states_out, token


def back_kernel(half_of, roles, sets, me_ref, q_ref, k_ref, v_ref, token_ref, *refs):
    normed_ref, gq_ref, gk_ref, gv_ref, done_ref, gq_buf, n_buf, gq_sem, n_sem = refs[-9:]
    length = q_ref.shape[0]
    rows = lax.broadcasted_iota(jnp.int32, (length, length), 0)
    columns = lax.broadcasted_iota(jnp.int32, (length, length), 1)
    mask, mask_t = columns <= rows, rows <= columns
    heads = gk_ref.shape[1] // DH
    half = half_of(me_ref[0])

    def chosen(index, place):
        value = refs[index][place]
        if sets > 1:
            value = jnp.where(among(me_ref[0], roles), refs[3 + index][place], value)
        return value

    n_buf[...] = chosen(0, (slice(None), slice(None)))
    normed_copy = half_copy(half, n_buf, normed_ref, n_sem)
    normed_copy.start()
    for h in range(heads):
        cols = half_columns(half, h, heads)
        q, k, v = (ref[:, cols] for ref in (q_ref, k_ref, v_ref))
        grad = chosen(1, (slice(None), head(h)))
        earlier = chosen(2, (head(h), slice(None)))
        scores_t = jnp.where(mask_t, dot_nt(k, q), 0.0).astype(BF16)
        grad_scores = jnp.where(mask, dot_nt(grad, v), 0.0).astype(BF16)
        grad_scores_t = jnp.where(mask_t, dot_nt(v, grad), 0.0).astype(BF16)
        gq_buf[:, head(h)] = (dot_nn(grad_scores, k) + dot_nt(grad, earlier)).astype(BF16)
        gk_ref[:, head(h)] = dot_nn(grad_scores_t, q)
        gv_ref[:, head(h)] = dot_nn(scores_t, grad)
    done_ref[...] = token_ref[...]
    gq_copy = half_copy(half, gq_buf, gq_ref, gq_sem)
    gq_copy.start()
    normed_copy.wait()
    gq_copy.wait()


def back(half_of, roles, me, q, k, v, token, sets, filled=()):
    length, width = q.shape
    whole = jax.ShapeDtypeStruct(q.shape, BF16)
    half_shape = jax.ShapeDtypeStruct((length, width // 2), F32)
    first = 5 + 3 * len(sets)
    buffers = pltpu.VMEM((length, width // 2), BF16)
    return pl.pallas_call(
        functools.partial(back_kernel, half_of, roles, len(sets)),
        in_specs=[SMEM_SPEC] + [VMEM_SPEC] * (first - 1) + [HBM_SPEC] * len(filled),
        out_specs=(HBM_SPEC, HBM_SPEC, VMEM_SPEC, VMEM_SPEC, VMEM_SPEC),
        scratch_shapes=[buffers, buffers] + [pltpu.SemaphoreType.DMA] * 2,
        input_output_aliases={first: 0, first + 1: 1} if filled else {},
        **params("back", (whole, whole, half_shape, half_shape, TOKEN)),
    )(me, q, k, v, token, *(x for one in sets for x in one), *filled)


def post_first_kernel(half_of, parts, *refs):
    refs[-5][...] = refs[5][...]
    post_kernel(half_of, parts, *refs[:-5], *refs[-4:])


def post_kernel(half_of, parts, me_ref, k_ref, v_ref, gk_in_ref, gv_in_ref, token_ref, *refs):
    l_refs, (gk_ref, gv_ref, gk_buf, gv_buf, gk_sem, gv_sem) = refs[:parts], refs[-6:]
    heads = gk_in_ref.shape[1] // DH
    half = half_of(me_ref[0])
    laters = [total(l_refs, head(h)) for h in range(heads)]
    for h in range(heads):
        k = k_ref[:, half_columns(half, h, heads)]
        gv_buf[:, head(h)] = (gv_in_ref[:, head(h)] + dot_nn(k, laters[h])).astype(BF16)
    gv_copy = half_copy(half, gv_buf, gv_ref, gv_sem)
    gv_copy.start()
    for h in range(heads):
        v = v_ref[:, half_columns(half, h, heads)]
        gk_buf[:, head(h)] = (gk_in_ref[:, head(h)] + dot_nt(v, laters[h])).astype(BF16)
    gk_copy = half_copy(half, gk_buf, gk_ref, gk_sem)
    gk_copy.start()
    gk_copy.wait()
    gv_copy.wait()


def post(half_of, me, k, v, gk_in, gv_in, token, later, filled=()):
    length, width = k.shape
    first = 6 + len(later)
    whole = jax.ShapeDtypeStruct(k.shape, BF16)
    return pl.pallas_call(
        functools.partial(post_kernel if filled else post_first_kernel, half_of, len(later)),
        in_specs=[SMEM_SPEC] + [VMEM_SPEC] * (first - 1) + [HBM_SPEC] * len(filled),
        out_specs=(HBM_SPEC, HBM_SPEC) if filled else (HBM_SPEC, HBM_SPEC, VMEM_SPEC),
        scratch_shapes=[pltpu.VMEM((length, width // 2), BF16)] * 2 + [pltpu.SemaphoreType.DMA] * 2,
        input_output_aliases={first: 0, first + 1: 1} if filled else {},
        **params("post", (whole, whole) if filled else (whole, whole, TOKEN)),
    )(me, k, v, gk_in, gv_in, token, *later, *filled)


def even_half(me):
    return 1 - lax.rem(me, 2)


def odd_half(me):
    return lax.rem(me, 2)


def rows_of(array):
    return array.reshape(array.shape[1:])


def shards_four(queries, key_vectors, value_vectors, grad_output):
    out_shape = queries.shape
    q, k, v, g = (rows_of(x) for x in (queries, key_vectors, value_vectors, grad_output))
    me = lax.axis_index("ctx").astype(jnp.int32).reshape(1)
    token = jnp.zeros(TOKEN.shape, TOKEN.dtype)

    def send(x, pairs):
        return lax.ppermute(x, "ctx", pairs)

    s_a, s_kept, token = states((0, 1), (0,), me, k, v, token)
    r_a = send(s_a, [(0, 1)])
    s_b, token = states((1,), (1,), me, k, v, token, (0,), (s_kept,))
    r_b = send(s_b, [(1, 2)])
    s_c, token = near_states(0, (1, 2), me, k, v, token, (0,), (s_b,))
    r_c = send(s_c, [(0, 2), (2, 3)])
    intra_out, qt, token = intra(q, k, v, token)
    shared = (q, qt, g, intra_out)
    s12, token = add(token, r_a, s_c)
    r_far = send(s12, [(1, 3)])
    s_y, token, s12 = near_states(1, (2,), me, k, v, token, passed=(s12,))
    r_near = send(s12, [(0, 1), (1, 2)])
    r_b, token = add(token, r_b)
    s123, token = add(token, r_b, r_c, s_y)
    r_last = send(s123, [(2, 3)])
    first_end, g_one, token = mid(even_half, (3,), me, shared, token, (r_c, r_far))
    u_one = send(g_one, [(3, 2)])
    first, g_first, token = mid(even_half, (0, 1, 2), me, shared, token, (r_a, r_b, r_c))
    u_side = send(g_first, [(2, 1)])
    second, g_rest, token = mid(odd_half, (0, 1, 2), me, shared, token, (r_near,))
    second_end, g_two, g_second, token = mid(odd_half, (3,), me, shared, token, (r_last,), (1,), (g_first, g_rest))
    u_two = send(g_two, [(3, 1), (1, 0)])
    normed, grad_q, gk_second, gv_second, token = back(odd_half, (3,), me, q, k, v, token, (second, second_end))
    g12, token = add(token, u_one, g_second)
    w_far = send(g12, [(2, 0)])
    w_near = send(g12, [(3, 2), (2, 1)])
    g123, token = add(token, u_side, u_two, g_second)
    w_last = send(g123, [(1, 0)])
    normed, grad_q, gk_first, gv_first, token = back(
        even_half, (3,), me, q, k, v, token, (first, first_end), (normed, grad_q)
    )
    *filled, token = post(odd_half, me, k, v, gk_second, gv_second, token, (u_one, u_side, u_two, w_far))
    l_near, token = add(token, w_near)
    grad_k, grad_v = post(even_half, me, k, v, gk_first, gv_first, token, (l_near, w_last), filled)
    return tuple(x.reshape(out_shape) for x in (normed, grad_q, grad_k, grad_v))


def scan_states(first, second, count, backward):
    rows = first.shape[0] * 2
    shares = jnp.concatenate([first, second], axis=0).reshape(count, rows // count, DH)
    shares = lax.all_to_all(shares, "ctx", split_axis=0, concat_axis=0, tiled=True).astype(F32)
    running = jnp.cumsum(shares, axis=0)
    sums = running[-1:] - running if backward else running - shares
    sums = lax.all_to_all(sums.astype(BF16), "ctx", split_axis=0, concat_axis=0, tiled=True)
    sums = sums.reshape(rows, DH)
    return sums[: rows // 2], sums[rows // 2 :]


def low_half(me):
    return 0


def high_half(me):
    return 1


def shards_any(count, queries, key_vectors, value_vectors, grad_output):
    out_shape = queries.shape
    q, k, v, g = (rows_of(x) for x in (queries, key_vectors, value_vectors, grad_output))
    me = lax.axis_index("ctx").astype(jnp.int32).reshape(1)
    token = jnp.zeros(TOKEN.shape, TOKEN.dtype)
    s1, token = near_states(0, (), me, k, v, token)
    s2, token = near_states(1, (), me, k, v, token)
    e1, e2 = scan_states(s1, s2, count, False)
    intra_out, qt, token = intra(q, k, v, token)
    shared = (q, qt, g, intra_out)
    low, g1, token = mid(low_half, (), me, shared, token, (e1,))
    high, g2, token = mid(high_half, (), me, shared, token, (e2,))
    l1, l2 = scan_states(g1, g2, count, True)
    normed, grad_q, gk1, gv1, token = back(low_half, (), me, q, k, v, token, (low,))
    normed, grad_q, gk2, gv2, token = back(high_half, (), me, q, k, v, token, (high,), (normed, grad_q))
    *filled, token = post(low_half, me, k, v, gk1, gv1, token, (l1,))
    grad_k, grad_v = post(high_half, me, k, v, gk2, gv2, token, (l2,), filled)
    return tuple(x.reshape(out_shape) for x in (normed, grad_q, grad_k, grad_v))


def solution(mesh):
    placed = P(("groups", "dp"), "ctx", "tp")
    count = mesh.shape["ctx"]

    def shards(*args):
        if count == 4:
            return shards_four(*args)
        return shards_any(count, *args)

    return jax.shard_map(
        shards,
        mesh=mesh,
        in_specs=(placed,) * 4,
        out_specs=(placed,) * 4,
        check_vma=False,
    )
```
